512 devices in a mesh: dom: 16 (over z, core), tile: 8 (over y), rep: 4 (over x).
Axes of the slice: x: 4, y: 8, z: 8, core: 2. Of those that a mesh axis runs over, the one named last changes fastest.
Arguments:
- quantizer_codes: int32 [131072, 32], P(('dom', 'tile', 'rep')), may hold values from 0 to 255
- codebook: bfloat16 [32, 256, 8], replicated, may hold values from -6 to 6
- adj_tiles: bfloat16 [512, 4, 256, 256], P(('dom', 'tile', 'rep')), may hold values from -0.3125 to 0.3125
- tile_list: int32 [512, 4, 2], P(('dom', 'tile', 'rep')), may hold values from 0 to 511, as said below
- tile_count: int32 [512], P(('dom', 'tile', 'rep')), may hold values from 1 to 4, as said below
- w_self: bfloat16 [256, 256], replicated, may hold values from -0.375 to 0.375
- w_neigh: bfloat16 [256, 256], replicated, may hold values from -0.375 to 0.375
- out_bias: float32 [256], replicated, may hold values from -3 to 3
- cotangent: bfloat16 [131072, 256], P(('dom', 'tile', 'rep')), may hold values from -0.15625 to 0.15625
Outputs:
- node_out: bfloat16 [131072, 256], P(('dom', 'tile', 'rep'))
- grad_self: float32 [256, 256], replicated
- grad_neigh: float32 [256, 256], replicated
- grad_bias: float32 [256], replicated
- grad_codebook: float32 [32, 256, 8], replicated
The draws below stay inside these ranges and needn't reach their ends.
Inputs may be any that keep to these rules, and one draw needn't show every extreme that they name: `tile_list`: for device i (index along dom+tile+rep), every slot's row block r has r % 32 == i % 32 and its column block c has c // 32 == i // 32; slots at or beyond tile_count[i] are ignored. `tile_count`: some device has exactly 4 live slots.
All inputs are finite; a program needn't handle non-finite values.
Results may differ from the reference program's by a relative error of at most 0.0055.
Values may be sent and summed in bfloat16 or wider, within the bound.
No kernel may reach another device: no remote copies, remote signals or barrier semaphores. Data moves between devices by JAX's collectives and lax.ppermute only.
A program may use at most 192 MiB of HBM per device.

```python
import jax
import jax.numpy as jnp
from jax import lax

B = 256
F = 256
SUBVECTOR_COUNT = 32
CENTROID_COUNT = 256
TSLOT = 4
SUBVECTOR_WIDTH = 8
BLOCKS = 512
GROUP = 32
DOMS = 16
GRAPH_NODES = 131072


def draw_tile_list(key, part):
    reader = jnp.arange(BLOCKS, dtype=jnp.int32)[:, None]
    row_dom = jax.random.randint(jax.random.fold_in(key, 11), (BLOCKS, TSLOT), 0, DOMS, dtype=jnp.int32)
    col_pos = jax.random.randint(jax.random.fold_in(key, 12), (BLOCKS, TSLOT), 0, GROUP, dtype=jnp.int32)
    row_ids = row_dom * GROUP + reader % GROUP
    col_ids = reader // GROUP * GROUP + col_pos
    return jnp.stack([row_ids, col_ids], axis=-1).astype(jnp.int32)


def draw_tile_count(key, part):
    base_count = 1 + jax.random.randint(jax.random.fold_in(key, 21), (BLOCKS,), 0, max(TSLOT // 2, 1), dtype=jnp.int32)
    busy_rows = jax.random.randint(jax.random.fold_in(key, 22), (BLOCKS,), 0, 8, dtype=jnp.int32) == 0
    forced_at = jax.random.randint(jax.random.fold_in(key, 23), (), 0, BLOCKS, dtype=jnp.int32)
    forced_row = jnp.arange(BLOCKS, dtype=jnp.int32) == forced_at
    return jnp.where(busy_rows | forced_row, TSLOT, base_count).astype(jnp.int32)


def plant(values, own_key, smallest, high):
    longest = values.shape.index(max(values.shape))
    spots = []
    for shift in (0, 1):
        where = [jax.random.randint(jax.random.fold_in(own_key, axis), (), 0, length) for axis, length in enumerate(values.shape)]
        where[longest] = (where[longest] + shift) % values.shape[longest]
        spots.append(tuple(where))
    return values.at[spots[0]].set(smallest).at[spots[1]].set(high)


def steps_of(stream_key, shape, split, smallest, high):
    loudness, own = 1.0, jax.random.fold_in(stream_key, 6)
    for axis_at, shards_of in split:
        heights = jnp.exp(jax.random.uniform(jax.random.fold_in(own, axis_at), (shards_of,), jnp.float32, smallest / len(split), high / len(split)))
        loudness = loudness * jnp.repeat(heights, shape[axis_at] // shards_of).reshape([-1 if axis == axis_at else 1 for axis in range(len(shape))])
    return loudness


def normal_values(stream_key, extent, spread, most, pieces=(), held_as=jnp.bfloat16):
    entries = jax.random.normal(stream_key, extent, jnp.float32) * spread
    if len(pieces) > 0:
        entries = steps_of(stream_key, extent, pieces, -0.22, 0.18) * entries
    return jnp.clip(entries, min=-most, max=most).astype(held_as)


def setup_inputs(seed: int = 0) -> dict:
    splits = jax.random.split(jax.random.key(seed), 10)
    return {
        "quantizer_codes": plant(jax.random.randint(splits[0], (GRAPH_NODES, SUBVECTOR_COUNT), 0, CENTROID_COUNT), jax.random.fold_in(splits[0], 1), 0, CENTROID_COUNT - 1).astype(jnp.int32),
        "codebook": normal_values(splits[1], (SUBVECTOR_COUNT, CENTROID_COUNT, SUBVECTOR_WIDTH), 1.0, 6.0),
        "adj_tiles": normal_values(splits[2], (BLOCKS, TSLOT, B, B), (B * TSLOT // 3) ** -0.5, 0.3125, ((0, 512),)),
        "tile_list": draw_tile_list(jax.random.fold_in(splits[9], 71), 0),
        "tile_count": draw_tile_count(jax.random.fold_in(splits[9], 71), 0),
        "w_self": normal_values(splits[5], (F, F), F ** -0.5, 0.375),
        "w_neigh": normal_values(splits[6], (F, F), F ** -0.5, 0.375),
        "out_bias": normal_values(splits[7], (F,), 0.5, 3.0, (), jnp.float32),
        "cotangent": normal_values(splits[8], (GRAPH_NODES, F), (4.0 / GRAPH_NODES ** 0.5), 0.15625, ((0, 512),)),
    }


def finish(pre_act):
    hidden = jax.nn.silu(pre_act)
    return hidden * lax.rsqrt(lax.optimization_barrier(jnp.mean(hidden * hidden, axis=-1, keepdims=True)) + 1e-05)

def reference(quantizer_codes, codebook, adj_tiles, tile_list, tile_count, w_self, w_neigh, out_bias, cotangent):
    subvector_index = jnp.arange(SUBVECTOR_COUNT, dtype=jnp.int32)[None, :]
    feats = codebook[subvector_index, quantizer_codes].reshape(GRAPH_NODES, F)
    feat_blocks = feats.reshape(BLOCKS, B, F)
    row_ids = tile_list[:, :, 0]
    col_ids = tile_list[:, :, 1]
    readers = jnp.arange(BLOCKS, dtype=jnp.int32)

    def forward_reader(running, scan_item):
        tile_data, rows_here, cols_here, live_count = scan_item

        def add_tile(slot_at, totals):
            product = jnp.dot(tile_data[slot_at], feat_blocks[cols_here[slot_at]], preferred_element_type=jnp.float32)
            return totals.at[rows_here[slot_at]].add(product)
        return (lax.fori_loop(jnp.int32(0), live_count, add_tile, running), None)
    aggregate, _ = lax.scan(forward_reader, jnp.zeros((BLOCKS, B, F), jnp.float32), (adj_tiles, row_ids, col_ids, tile_count))
    agg_low = aggregate.reshape(GRAPH_NODES, F).astype(jnp.bfloat16)
    pre_act = jnp.dot(feats, w_self, preferred_element_type=jnp.float32) + jnp.dot(agg_low, w_neigh, preferred_element_type=jnp.float32) + out_bias
    out_full, pullback = jax.vjp(finish, pre_act)
    node_out = out_full.astype(jnp.bfloat16)
    dpre = pullback(cotangent.astype(jnp.float32))[0].astype(jnp.bfloat16)
    grad_self = jnp.dot(feats.T, dpre, preferred_element_type=jnp.float32)
    grad_neigh = jnp.dot(agg_low.T, dpre, preferred_element_type=jnp.float32)
    grad_bias = lax.optimization_barrier(jnp.sum(dpre.astype(jnp.float32), axis=0))
    dx_self = jnp.dot(dpre, w_self.T, preferred_element_type=jnp.float32)
    dagg = jnp.dot(dpre, w_neigh.T, preferred_element_type=jnp.float32).astype(jnp.bfloat16).reshape(BLOCKS, B, F)

    def backward_reader(running, scan_item):
        tile_data, rows_here, cols_here, live_count, reader = scan_item
        first_col = reader // GROUP * GROUP

        def add_tile(slot_at, totals):
            product = jnp.dot(tile_data[slot_at].T, dagg[rows_here[slot_at]], preferred_element_type=jnp.float32)
            return totals.at[cols_here[slot_at] - first_col].add(product)
        column = lax.fori_loop(jnp.int32(0), live_count, add_tile, jnp.zeros((GROUP, B, F), jnp.float32))
        column = lax.optimization_barrier(column.astype(jnp.bfloat16)).astype(jnp.float32)
        current = lax.dynamic_slice_in_dim(running, first_col, GROUP, 0) + column
        return (lax.dynamic_update_slice_in_dim(running, current, first_col, 0), None)
    dx_neigh, _ = lax.scan(backward_reader, jnp.zeros((BLOCKS, B, F), jnp.float32), (adj_tiles, row_ids, col_ids, tile_count, readers))
    input_gradient_total = dx_self + dx_neigh.reshape(GRAPH_NODES, F)
    per_subvector = input_gradient_total.reshape(GRAPH_NODES, SUBVECTOR_COUNT, SUBVECTOR_WIDTH)
    grad_codebook = jax.vmap(lambda sub_grads, sub_codes: jax.ops.segment_sum(sub_grads, sub_codes, num_segments=CENTROID_COUNT), in_axes=(1, 1))(per_subvector, quantizer_codes)
    return (node_out, grad_self, grad_neigh, grad_bias, grad_codebook)
```

```python
import functools

import jax
import jax.numpy as jnp
from jax import lax
from jax.experimental import pallas as pl
from jax.experimental.pallas import tpu as pltpu
from jax.sharding import PartitionSpec as P

INTERPRET = False
F32 = jnp.float32
BF16 = jnp.bfloat16
VM = pltpu.VMEM
DOM = ("dom",)
PLANE = ("tile", "rep")


def contract(a, b, da, db):
    return lax.dot_general(a, b, (((da,), (db,)), ((), ())), preferred_element_type=F32)


def call(kernel, name, out_shape, scalars, arrays, scratch=()):
    return pl.pallas_call(
        kernel,
        name=name,
        out_shape=out_shape,
        in_specs=[pl.BlockSpec(memory_space=pltpu.SMEM)] * len(scalars)
        + [pl.BlockSpec(memory_space=VM)] * len(arrays),
        out_specs=jax.tree.map(lambda _: pl.BlockSpec(memory_space=VM), out_shape),
        scratch_shapes=list(scratch),
        interpret=INTERPRET,
    )(*scalars, *arrays)


def struct(shape, dtype):
    return jax.ShapeDtypeStruct(shape, dtype)


def onehot(row, centroid_ids):
    return jnp.where(centroid_ids == row, 1.0, 0.0).astype(BF16)


def centroid_iota(centroids, nodes):
    return lax.broadcasted_iota(jnp.int32, (centroids, nodes), 0).astype(F32)


def decode(codes, book_ref, ids, out_ref):
    sub_count, width, _ = book_ref.shape
    for m in range(sub_count):
        hot = onehot(codes[m : m + 1, :], ids)
        out_ref[m * width : (m + 1) * width, :] = jnp.dot(
            book_ref[m], hot, preferred_element_type=F32
        ).astype(out_ref.dtype)


def pack_kernel(tl_ref, tc_ref, codes_ref, cot_ref, spread_ref, side_ref):
    plane, subs, nodes = spread_ref.shape
    doms, rows2, width = side_ref.shape
    rows = rows2 // 2
    slots = tl_ref.shape[1]
    group = 128 // (slots * rows)
    codes = codes_ref[...].astype(F32).astype(BF16)
    spread_ref[...] = jnp.broadcast_to(codes[None], (plane, subs, nodes))
    eye = (
        lax.broadcasted_iota(jnp.int32, (subs, 128), 0)
        == lax.broadcasted_iota(jnp.int32, (subs, 128), 1)
    ).astype(F32)
    code_rows = contract(codes, eye.astype(BF16), 0, 0).astype(BF16)
    lane = lax.broadcasted_iota(jnp.int32, (rows, 128), 1)
    me = lax.axis_index("dom")
    at = lane - (me % group) * (slots * rows)
    slot = at // rows
    meta = jnp.zeros((rows, 128), jnp.int32)
    for s in range(slots):
        target = tl_ref[0, s] // plane * rows
        live = s < tc_ref[0]
        here = (at >= s * rows) & (at < (s + 1) * rows)
        meta = jnp.where(here, jnp.where(live, target + at - s * rows, nodes), meta)
    meta = meta.astype(F32).astype(BF16)
    for j in range(doms):
        side_ref[j, 0:rows, :] = cot_ref[j * rows : (j + 1) * rows, :]
        side_ref[j, rows:rows2, 0:128] = code_rows[j * rows : (j + 1) * rows, :]
        side_ref[j, rows:rows2, 128:256] = meta


def forward_kernel(tl_ref, adj_ref, codes_ref, book_ref, out_ref, feats_ref):
    plane = codes_ref.shape[0]
    doms = out_ref.shape[0]
    slots, side, _ = adj_ref.shape
    rows = side // doms
    ids = centroid_iota(book_ref.shape[2], codes_ref.shape[2])
    for s in range(slots):
        codes = codes_ref[tl_ref[1, s] % plane].astype(F32)
        decode(codes, book_ref, ids, feats_ref)
        prod = contract(adj_ref[s], feats_ref[...].astype(BF16), 1, 1).astype(BF16)
        for j in range(doms):
            out_ref[j, s * rows : (s + 1) * rows, :] = prod[j * rows : (j + 1) * rows, :]


def own_kernel(side_ref, book_ref, w_ref, bias_ref, feats_out, pre_ref, codes_out, feats_ref):
    doms, rows2, _ = side_ref.shape
    rows = rows2 // 2
    subs = book_ref.shape[0]
    code_rows = side_ref[:, rows:rows2, 0:128].reshape(doms * rows, 128)
    eye = (
        lax.broadcasted_iota(jnp.int32, (subs, 128), 0)
        == lax.broadcasted_iota(jnp.int32, (subs, 128), 1)
    ).astype(F32)
    codes = contract(eye.astype(BF16), code_rows, 1, 1)
    codes_out[...] = codes
    ids = centroid_iota(book_ref.shape[2], codes.shape[1])
    decode(codes, book_ref, ids, feats_ref)
    feats = feats_ref[...].astype(BF16)
    feats_out[...] = feats
    pre_ref[...] = contract(feats, w_ref[...], 0, 0) + bias_ref[...]


def node_kernel(side_ref, part_ref, pre_ref, w_ref, need_ref, node_ref, dpre_ref, agg_ref):
    doms, rows2, width = side_ref.shape
    rows = rows2 // 2
    per = part_ref.shape[1]
    group = 128 // per
    nodes = doms * rows
    row_ids = lax.broadcasted_iota(jnp.int32, (nodes, 128), 0).astype(F32)
    picks = []
    total = jnp.zeros((nodes, width), F32)
    for g in range(doms // group):
        meta = side_ref[g * group, rows : rows + 1, 128:256].astype(F32)
        for b in range(1, group):
            meta = meta + side_ref[g * group + b, rows : rows + 1, 128:256].astype(F32)
        pick = jnp.where(row_ids == meta, 1.0, 0.0).astype(BF16)
        picks.append(pick)
        terms = part_ref[g * group : (g + 1) * group].reshape(128, width)
        total = total + jnp.dot(pick, terms, preferred_element_type=F32)
    agg = total.astype(BF16)
    agg_ref[...] = agg
    pre = pre_ref[...] + jnp.dot(agg, w_ref[...], preferred_element_type=F32)
    gate = 1.0 / (1.0 + jnp.exp(-pre))
    hidden = pre * gate
    inv = lax.rsqrt(jnp.mean(hidden * hidden, axis=-1, keepdims=True) + 1e-05)
    node_ref[...] = (hidden * inv).astype(BF16).reshape(node_ref.shape)
    cot = side_ref[:, 0:rows, :].reshape(nodes, width).astype(F32)
    lean = jnp.mean(cot * hidden, axis=-1, keepdims=True) * (inv * inv * inv)
    dhidden = cot * inv - hidden * lean
    dpre = (dhidden * gate * (1.0 + pre * (1.0 - gate))).astype(BF16)
    dpre_ref[...] = dpre
    dagg = contract(dpre, w_ref[...], 1, 1).astype(BF16)
    for g in range(doms // group):
        need = contract(picks[g], dagg, 0, 0).astype(BF16)
        need_ref[g * group : (g + 1) * group] = need.reshape(group, per, width)


def weights_kernel(feats_ref, agg_ref, dpre_ref, w_ref, codes_ref, grads_ref, book_ref):
    plane, rows3, width = grads_ref.shape
    rows = rows3 - 8
    half = rows // 2
    dpre = dpre_ref[...]
    grad_self = jnp.dot(feats_ref[...], dpre, preferred_element_type=F32)
    grad_neigh = contract(agg_ref[...], dpre, 0, 0)
    bias = jnp.sum(dpre.astype(F32), axis=0, keepdims=True)
    for j in range(plane):
        grads_ref[j, 0:half, :] = grad_self[j * half : (j + 1) * half, :]
        grads_ref[j, half:rows, :] = grad_neigh[j * half : (j + 1) * half, :]
        grads_ref[j, rows:rows3, :] = jnp.broadcast_to(bias, (8, width))
    dx = contract(w_ref[...], dpre, 1, 1)
    subs, sub_width, centroids = book_ref.shape
    ids = centroid_iota(centroids, codes_ref.shape[1])
    high = dx.astype(BF16)
    low = (dx - high.astype(F32)).astype(BF16)
    for m in range(subs):
        hot = onehot(codes_ref[m : m + 1, :], ids)
        at = slice(m * sub_width, (m + 1) * sub_width)
        book_ref[m] = contract(high[at], hot, 1, 1) + contract(low[at], hot, 1, 1)


def backward_kernel(tl_ref, need_ref, adj_ref, codes_ref, own_ref, out_ref, dx_ref):
    plane = codes_ref.shape[0]
    slots, side, _ = adj_ref.shape
    subs, sub_width, centroids = out_ref.shape
    doms, per, width = need_ref.shape
    rows = per // slots
    ids = centroid_iota(centroids, codes_ref.shape[2])
    out_ref[...] = own_ref[...]
    for s in range(slots):
        dagg = need_ref[:, s * rows : (s + 1) * rows, :].reshape(side, width)
        dx_ref[...] = contract(dagg, adj_ref[s], 0, 0).astype(BF16).astype(F32)
        codes = codes_ref[tl_ref[1, s] % plane].astype(F32)
        for m in range(subs):
            hot = onehot(codes[m : m + 1, :], ids)
            dx = dx_ref[m * sub_width : (m + 1) * sub_width, :].astype(BF16)
            out_ref[m] += contract(dx, hot, 1, 1)


def sum_spread_kernel(in_ref, out_ref):
    total = jnp.sum(in_ref[...], axis=0)
    out_ref[...] = jnp.broadcast_to(total[None], out_ref.shape)


def exchange(x, axes):
    return lax.all_to_all(x, axes, split_axis=0, concat_axis=0, tiled=True)


def sum_everywhere(pieces, doms, name):
    plane = pieces.shape[0]
    tail = pieces.shape[1:]
    got = exchange(pieces, PLANE)
    got = exchange(call(sum_spread_kernel, name + "_a", struct((doms, *tail), F32), (), (got,)), DOM)
    got = call(sum_spread_kernel, name + "_b", struct((plane, *tail), F32), (), (got,))
    return exchange(got, PLANE)


def body(quantizer_codes, codebook, adj_tiles, tile_list, tile_count, w_self, w_neigh, out_bias, cotangent):
    doms = lax.axis_size("dom")
    plane = lax.axis_size("tile") * lax.axis_size("rep")
    subs, centroids, sub_width = codebook.shape
    slots, side = adj_tiles.shape[1:3]
    width = subs * sub_width
    rows = side // doms
    codes = quantizer_codes.T
    book = codebook.transpose(0, 2, 1)
    adj = adj_tiles[0]
    slot_ids = tile_list[0].T
    bias = out_bias.reshape(1, width)

    spread, side_pay = call(
        pack_kernel, "pack",
        (struct((plane, subs, side), BF16), struct((doms, 2 * rows, width), BF16)),
        (slot_ids, tile_count), (codes, cotangent),
    )
    all_codes = exchange(spread, PLANE)
    side_got = exchange(side_pay, DOM)
    parts = call(
        forward_kernel, "forward", struct((doms, slots * rows, width), BF16),
        (slot_ids,), (adj, all_codes, book), (VM((width, side), F32),),
    )
    parts = exchange(parts, DOM)
    feats, pre_self, own_codes = call(
        own_kernel, "own",
        (struct((width, side), BF16), struct((side, width), F32), struct((subs, side), F32)),
        (), (side_got, book, w_self, bias), (VM((width, side), F32),),
    )
    need, node, dpre, agg = call(
        node_kernel, "node",
        (struct((doms, slots * rows, width), BF16), struct((doms, rows, width), BF16),
         struct((side, width), BF16), struct((side, width), BF16)),
        (), (side_got, parts, pre_self, w_neigh),
    )
    need = exchange(need, DOM)
    half = width // plane
    grads, own_book = call(
        weights_kernel, "weights",
        (struct((plane, 2 * half + 8, width), F32), struct((subs, sub_width, centroids), F32)),
        (), (feats, agg, dpre, w_self, own_codes),
    )
    grads = sum_everywhere(grads, doms, "grads")
    book_part = call(
        backward_kernel, "backward", struct((subs, sub_width, centroids), F32),
        (slot_ids,), (need, adj, all_codes, own_book), (VM((width, side), F32),),
    )
    node_out = exchange(node, DOM).reshape(side, width)
    grad_book = sum_everywhere(
        book_part.reshape(plane, subs * sub_width // plane, centroids), doms, "book"
    ).reshape(subs, sub_width, centroids)
    grad_self = grads[:, 0:half, :].reshape(width, width)
    grad_neigh = grads[:, half : 2 * half, :].reshape(width, width)
    grad_bias = grads[0, 2 * half, :]
    return (node_out, grad_self, grad_neigh, grad_bias, grad_book.transpose(0, 2, 1))


def solution(mesh):
    every = ("dom", "tile", "rep")
    in_specs = (
        P(every, None), P(), P(every, None, None, None), P(every, None, None), P(every),
        P(), P(), P(), P(every, None),
    )
    out_specs = (P(every, None), P(), P(), P(), P())
    return jax.shard_map(body, mesh=mesh, in_specs=in_specs, out_specs=out_specs, check_vma=False)
```

```python
import functools

import jax
import jax.numpy as jnp
from jax import lax
from jax.experimental import pallas as pl
from jax.experimental.pallas import tpu as pltpu
from jax.sharding import PartitionSpec as P

INTERPRET = False
F32 = jnp.float32
BF16 = jnp.bfloat16
VM = pltpu.VMEM
DOM = ("dom",)
PLANE = ("tile", "rep")


def contract(a, b, da, db):
    return lax.dot_general(a, b, (((da,), (db,)), ((), ())), preferred_element_type=F32)


def call(kernel, name, out_shape, scalars, arrays, scratch=()):
    return pl.pallas_call(
        kernel,
        name=name,
        out_shape=out_shape,
        in_specs=[pl.BlockSpec(memory_space=pltpu.SMEM)] * len(scalars)
        + [pl.BlockSpec(memory_space=VM)] * len(arrays),
        out_specs=jax.tree.map(lambda _: pl.BlockSpec(memory_space=VM), out_shape),
        scratch_shapes=list(scratch),
        interpret=INTERPRET,
    )(*scalars, *arrays)


def struct(shape, dtype):
    return jax.ShapeDtypeStruct(shape, dtype)


def onehot(row, centroid_ids):
    return jnp.where(centroid_ids == row, 1.0, 0.0).astype(BF16)


def centroid_iota(centroids, nodes):
    return lax.broadcasted_iota(jnp.int32, (centroids, nodes), 0).astype(F32)


def decode(codes, book_ref, ids, out_ref):
    sub_count, width, _ = book_ref.shape
    for m in range(sub_count):
        hot = onehot(codes[m : m + 1, :], ids)
        out_ref[m * width : (m + 1) * width, :] = jnp.dot(
            book_ref[m], hot, preferred_element_type=F32
        ).astype(out_ref.dtype)


def side_kernel(plane, tl_ref, tc_ref, codes_ref, cot_ref, side_ref):
    doms, rows2, width = side_ref.shape
    rows = rows2 // 2
    subs, nodes = codes_ref.shape
    slots = tl_ref.shape[1]
    group = 128 // (slots * rows)
    codes = codes_ref[...].astype(F32).astype(BF16)
    eye = (
        lax.broadcasted_iota(jnp.int32, (subs, 128), 0)
        == lax.broadcasted_iota(jnp.int32, (subs, 128), 1)
    ).astype(F32)
    code_rows = contract(codes, eye.astype(BF16), 0, 0).astype(BF16)
    at = lax.broadcasted_iota(jnp.int32, (rows, 128), 1)
    at = at - (lax.axis_index("dom") % group) * (slots * rows)
    meta = jnp.zeros((rows, 128), jnp.int32)
    for s in range(slots):
        target = tl_ref[0, s] // plane * rows
        here = (at >= s * rows) & (at < (s + 1) * rows)
        live = s < tc_ref[0]
        meta = jnp.where(here, jnp.where(live, target + at - s * rows, nodes), meta)
    meta = meta.astype(F32).astype(BF16)
    for j in range(doms):
        side_ref[j, 0:rows, :] = cot_ref[j * rows : (j + 1) * rows, :]
        side_ref[j, rows:rows2, 0:128] = code_rows[j * rows : (j + 1) * rows, :]
        side_ref[j, rows:rows2, 128:256] = meta


def forward_kernel(tl_ref, adj_ref, codes_ref, book_ref, side_ref, out_ref, feats_ref):
    plane = codes_ref.shape[0]
    doms = out_ref.shape[0]
    slots, side, _ = adj_ref.shape
    rows = side // doms
    ids = centroid_iota(book_ref.shape[2], codes_ref.shape[2])
    for s in range(slots):
        codes = codes_ref[tl_ref[1, s] % plane].astype(F32)
        decode(codes, book_ref, ids, feats_ref)
        prod = contract(adj_ref[s], feats_ref[...].astype(BF16), 1, 1).astype(BF16)
        for j in range(doms):
            out_ref[j, s * rows : (s + 1) * rows, :] = prod[j * rows : (j + 1) * rows, :]
    out_ref[:, slots * rows :, :] = side_ref[...]


def node_kernel(
    got_ref, book_ref, wself_ref, wneigh_ref, bias_ref,
    send_ref, dpre_ref, agg_ref, feats_out, codes_out, feats_ref,
):
    doms, all_rows, width = got_ref.shape
    per = all_rows * 2 // 3
    rows = (all_rows - per) // 2
    group = 128 // per
    nodes = doms * rows
    subs = book_ref.shape[0]
    code_rows = got_ref[:, per + rows :, 0:128].reshape(nodes, 128)
    eye = (
        lax.broadcasted_iota(jnp.int32, (subs, 128), 0)
        == lax.broadcasted_iota(jnp.int32, (subs, 128), 1)
    ).astype(F32)
    codes = contract(eye.astype(BF16), code_rows, 1, 1)
    codes_out[...] = codes
    decode(codes, book_ref, centroid_iota(book_ref.shape[2], nodes), feats_ref)
    feats = feats_ref[...].astype(BF16)
    feats_out[...] = feats

    row_ids = lax.broadcasted_iota(jnp.int32, (nodes, 128), 0).astype(F32)
    picks = []
    total = jnp.zeros((nodes, width), F32)
    at = per + rows
    for g in range(doms // group):
        meta = got_ref[g * group, at : at + 1, 128:256].astype(F32)
        for b in range(1, group):
            meta = meta + got_ref[g * group + b, at : at + 1, 128:256].astype(F32)
        pick = jnp.where(row_ids == meta, 1.0, 0.0).astype(BF16)
        picks.append(pick)
        terms = got_ref[g * group : (g + 1) * group, 0:per, :].reshape(128, width)
        total = total + jnp.dot(pick, terms, preferred_element_type=F32)
    agg = total.astype(BF16)
    agg_ref[...] = agg
    pre = (
        contract(feats, wself_ref[...], 0, 0)
        + jnp.dot(agg, wneigh_ref[...], preferred_element_type=F32)
        + bias_ref[...]
    )
    gate = 1.0 / (1.0 + jnp.exp(-pre))
    hidden = pre * gate
    inv = lax.rsqrt(jnp.mean(hidden * hidden, axis=-1, keepdims=True) + 1e-05)
    send_ref[:, per:, :] = (hidden * inv).astype(BF16).reshape(doms, rows, width)
    cot = got_ref[:, per : per + rows, :].reshape(nodes, width).astype(F32)
    lean = jnp.mean(cot * hidden, axis=-1, keepdims=True) * (inv * inv * inv)
    dhidden = cot * inv - hidden * lean
    dpre = (dhidden * gate * (1.0 + pre * (1.0 - gate))).astype(BF16)
    dpre_ref[...] = dpre
    dagg = contract(dpre, wneigh_ref[...], 1, 1).astype(BF16)
    for g in range(doms // group):
        need = contract(picks[g], dagg, 0, 0).astype(BF16)
        send_ref[g * group : (g + 1) * group, 0:per, :] = need.reshape(group, per, width)


def weights_kernel(feats_ref, agg_ref, dpre_ref, w_ref, codes_ref, self_ref, neigh_ref, bias_ref, book_ref):
    dpre = dpre_ref[...]
    self_ref[...] = jnp.dot(feats_ref[...], dpre, preferred_element_type=F32)
    neigh_ref[...] = contract(agg_ref[...], dpre, 0, 0)
    bias = jnp.sum(dpre.astype(F32), axis=0, keepdims=True)
    bias_ref[...] = jnp.broadcast_to(bias, bias_ref.shape)
    dx = contract(w_ref[...], dpre, 1, 1)
    subs, sub_width, centroids = book_ref.shape
    ids = centroid_iota(centroids, codes_ref.shape[1])
    high = dx.astype(BF16)
    low = (dx - high.astype(F32)).astype(BF16)
    for m in range(subs):
        hot = onehot(codes_ref[m : m + 1, :], ids)
        at = slice(m * sub_width, (m + 1) * sub_width)
        book_ref[m] = contract(high[at], hot, 1, 1) + contract(low[at], hot, 1, 1)


def backward_kernel(
    tl_ref, got_ref, adj_ref, codes_ref, own_ref, self_ref, neigh_ref, bias_ref,
    keep_ref, give_ref, node_ref, dx_ref, book_ref,
):
    plane = codes_ref.shape[0]
    slots, side, _ = adj_ref.shape
    subs, sub_width, centroids = own_ref.shape
    doms, all_rows, width = got_ref.shape
    rows = side // doms
    per = slots * rows
    ids = centroid_iota(centroids, codes_ref.shape[2])
    book_ref[...] = own_ref[...]
    for s in range(slots):
        dagg = got_ref[:, s * rows : (s + 1) * rows, :].reshape(side, width)
        dx_ref[...] = contract(dagg, adj_ref[s], 0, 0).astype(BF16).astype(F32)
        codes = codes_ref[tl_ref[1, s] % plane].astype(F32)
        for m in range(subs):
            hot = onehot(codes[m : m + 1, :], ids)
            dx = dx_ref[m * sub_width : (m + 1) * sub_width, :].astype(BF16)
            book_ref[m] += contract(dx, hot, 1, 1)
    node_ref[...] = got_ref[:, per:, :].reshape(side, width)
    core = lax.axis_index("dom") % 2
    pieces = keep_ref.shape[0]
    half = width // pieces
    each = subs // pieces
    low = lax.broadcasted_iota(jnp.int32, (sub_width, centroids), 0) < sub_width // 2
    bias = bias_ref[...]

    def write(first_ref, second_ref):
        for j in range(pieces):
            first_ref[j, 0:half, :] = self_ref[j * half : (j + 1) * half, :]
            second_ref[j, 0:half, :] = neigh_ref[j * half : (j + 1) * half, :]
            for e in range(each):
                at = slice(half + e * sub_width, half + (e + 1) * sub_width)
                value = book_ref[j * each + e]
                first_ref[j, at, :] = jnp.where(low, value, bias)
                second_ref[j, at, :] = jnp.where(low, 0.0, value)

    @pl.when(core == 0)
    def _():
        write(keep_ref, give_ref)

    @pl.when(core == 1)
    def _():
        write(give_ref, keep_ref)


def pair_kernel(keep_ref, got_ref, out_ref):
    out_ref[...] = (keep_ref[...] + got_ref[...]).astype(out_ref.dtype)


def sum_spread_kernel(in_ref, out_ref):
    total = jnp.sum(in_ref[...].astype(F32), axis=0)
    out_ref[...] = jnp.broadcast_to(total[None].astype(out_ref.dtype), out_ref.shape)


def finish_kernel(mine_ref, other_ref, self_ref, neigh_ref, bias_ref, book_ref):
    core = lax.axis_index("dom") % 2
    pieces = mine_ref.shape[0]
    half = self_ref.shape[0] // pieces
    subs, sub_width, centroids = book_ref.shape
    each = subs // pieces
    low = lax.broadcasted_iota(jnp.int32, (sub_width, centroids), 0) < sub_width // 2

    def write(first_ref, second_ref):
        for j in range(pieces):
            first = first_ref[j].astype(F32)
            second = second_ref[j].astype(F32)
            self_ref[j * half : (j + 1) * half, :] = first[0:half]
            neigh_ref[j * half : (j + 1) * half, :] = second[0:half]
            for e in range(each):
                at = slice(half + e * sub_width, half + (e + 1) * sub_width)
                book_ref[j * each + e] = jnp.where(low, first[at], second[at])
        row = half + sub_width // 2
        bias_ref[...] = first_ref[0].astype(F32)[row : row + 1]

    @pl.when(core == 0)
    def _():
        write(mine_ref, other_ref)

    @pl.when(core == 1)
    def _():
        write(other_ref, mine_ref)


def exchange(x, axes, groups=None):
    return lax.all_to_all(x, axes, split_axis=0, concat_axis=0, tiled=True, axis_index_groups=groups)


def body(quantizer_codes, codebook, adj_tiles, tile_list, tile_count, w_self, w_neigh, out_bias, cotangent):
    doms = lax.axis_size("dom")
    plane = lax.axis_size("tile") * lax.axis_size("rep")
    subs, centroids, sub_width = codebook.shape
    slots, side = adj_tiles.shape[1:3]
    width = subs * sub_width
    rows = side // doms
    per = slots * rows
    codes = quantizer_codes.T
    book = codebook.transpose(0, 2, 1)
    adj = adj_tiles[0]
    slot_ids = tile_list[0].T
    bias = out_bias.reshape(1, width)
    swap = [(i, i ^ 1) for i in range(doms)]
    cores = [list(range(c, doms, 2)) for c in range(2)]

    spread = jnp.broadcast_to(codes.astype(BF16)[None], (plane, subs, side))
    all_codes = exchange(spread, PLANE)
    side_rows = call(
        functools.partial(side_kernel, plane), "side", struct((doms, 2 * rows, width), BF16),
        (slot_ids, tile_count), (codes, cotangent),
    )
    parts = call(
        forward_kernel, "forward", struct((doms, per + 2 * rows, width), BF16),
        (slot_ids,), (adj, all_codes, book, side_rows), (VM((width, side), F32),),
    )
    parts = exchange(parts, DOM)
    need, dpre, agg, feats, own_codes = call(
        node_kernel, "node",
        (struct((doms, per + rows, width), BF16), struct((side, width), BF16),
         struct((side, width), BF16), struct((width, side), BF16), struct((subs, side), F32)),
        (), (parts, book, w_self, w_neigh, bias), (VM((width, side), F32),),
    )
    need = exchange(need, DOM)
    grad_self, grad_neigh, grad_bias, own_book = call(
        weights_kernel, "weights",
        (struct((width, width), F32), struct((width, width), F32), struct((sub_width, width), F32),
         struct((subs, sub_width, centroids), F32)),
        (), (feats, agg, dpre, w_self, own_codes),
    )
    piece = (width + subs * sub_width) // plane
    keep, give, node_out = call(
        backward_kernel, "backward",
        (struct((plane, piece, width), F32), struct((plane, piece, width), F32), struct((side, width), BF16)),
        (slot_ids,), (need, adj, all_codes, own_book, grad_self, grad_neigh, grad_bias),
        (VM((width, side), F32), VM((subs, sub_width, centroids), F32)),
    )
    got = lax.ppermute(give, "dom", swap)
    half = call(pair_kernel, "pair", struct((plane, piece, width), BF16), (), (keep, got))
    half = exchange(half, PLANE)
    half = call(sum_spread_kernel, "sum_plane", struct((doms // 2, piece, width), F32), (), (half,))
    half = exchange(half, "dom", cores)
    half = call(sum_spread_kernel, "sum_dom", struct((plane, piece, width), BF16), (), (half,))
    mine = exchange(half, PLANE)
    other = lax.ppermute(mine, "dom", swap)
    grad_self, grad_neigh, grad_bias, grad_book = call(
        finish_kernel, "finish",
        (struct((width, width), F32), struct((width, width), F32), struct((1, width), F32),
         struct((subs, sub_width, centroids), F32)),
        (), (mine, other),
    )
    return (node_out, grad_self, grad_neigh, grad_bias.reshape(width), grad_book.transpose(0, 2, 1))


def solution(mesh):
    every = ("dom", "tile", "rep")
    in_specs = (
        P(every, None), P(), P(every, None, None, None), P(every, None, None), P(every),
        P(), P(), P(), P(every, None),
    )
    out_specs = (P(every, None), P(), P(), P(), P())
    return jax.shard_map(body, mesh=mesh, in_specs=in_specs, out_specs=out_specs, check_vma=False)
```

```python
import functools

import jax
import jax.numpy as jnp
from jax import lax
from jax.experimental import pallas as pl
from jax.experimental.pallas import tpu as pltpu
from jax.sharding import PartitionSpec as P

INTERPRET = False
F32 = jnp.float32
BF16 = jnp.bfloat16
VM = pltpu.VMEM
VMEM_LIMIT = 16 << 20
DOM = ("dom",)
PLANE = ("tile", "rep")


def contract(a, b, da, db):
    return lax.dot_general(a, b, (((da,), (db,)), ((), ())), preferred_element_type=F32)


def call(kernel, name, out_shape, scalars, arrays, scratch=(), final=0):
    if not INTERPRET:
        arrays = [pltpu.with_memory_space_constraint(a, VM) for a in arrays]
        shapes = out_shape if isinstance(out_shape, tuple) else (out_shape,)
        kept = len(shapes) - final
        shapes = tuple(VM(o.shape, o.dtype) if i < kept else o for i, o in enumerate(shapes))
        out_shape = shapes if isinstance(out_shape, tuple) else shapes[0]
    return pl.pallas_call(
        kernel,
        name=name,
        out_shape=out_shape,
        in_specs=[pl.BlockSpec(memory_space=pltpu.SMEM)] * len(scalars)
        + [pl.BlockSpec(memory_space=VM)] * len(arrays),
        out_specs=jax.tree.map(lambda _: pl.BlockSpec(memory_space=VM), out_shape),
        scratch_shapes=list(scratch),
        compiler_params=pltpu.CompilerParams(vmem_limit_bytes=VMEM_LIMIT),
        interpret=INTERPRET,
    )(*scalars, *arrays)


def struct(shape, dtype):
    return jax.ShapeDtypeStruct(shape, dtype)


def onehot(row, centroid_ids):
    return jnp.where(centroid_ids.astype(BF16) == row.astype(BF16), jnp.ones((), BF16), jnp.zeros((), BF16))


def centroid_iota(centroids, nodes):
    return lax.broadcasted_iota(jnp.int32, (centroids, nodes), 0).astype(F32)


def decode(codes, book_ref, ids, out_ref):
    sub_count, width, _ = book_ref.shape
    for m in range(sub_count):
        hot = onehot(codes[m : m + 1, :], ids)
        out_ref[m * width : (m + 1) * width, :] = jnp.dot(
            book_ref[m], hot, preferred_element_type=F32
        ).astype(out_ref.dtype)


def side_kernel(plane, tl_ref, tc_ref, codes_ref, cot_ref, side_ref):
    doms, rows2, width = side_ref.shape
    rows = rows2 // 2
    subs, nodes = codes_ref.shape
    slots = tl_ref.shape[1]
    group = 128 // (slots * rows)
    codes = codes_ref[...].astype(F32).astype(BF16)
    eye = (
        lax.broadcasted_iota(jnp.int32, (subs, 128), 0)
        == lax.broadcasted_iota(jnp.int32, (subs, 128), 1)
    ).astype(F32)
    code_rows = contract(codes, eye.astype(BF16), 0, 0).astype(BF16)
    at = lax.broadcasted_iota(jnp.int32, (rows, 128), 1)
    at = at - (lax.axis_index("dom") % group) * (slots * rows)
    meta = jnp.zeros((rows, 128), jnp.int32)
    for s in range(slots):
        target = tl_ref[0, s] // plane * rows
        here = (at >= s * rows) & (at < (s + 1) * rows)
        live = s < tc_ref[0]
        meta = jnp.where(here, jnp.where(live, target + at - s * rows, nodes), meta)
    meta = meta.astype(F32).astype(BF16)
    for j in range(doms):
        side_ref[j, 0:rows, :] = cot_ref[j * rows : (j + 1) * rows, :]
        side_ref[j, rows:rows2, 0:128] = code_rows[j * rows : (j + 1) * rows, :]
        side_ref[j, rows:rows2, 128:256] = meta


def forward_kernel(tl_ref, adj_ref, codes_ref, book_ref, side_ref, out_ref, feats_ref):
    plane = codes_ref.shape[0]
    doms = out_ref.shape[0]
    slots, side, _ = adj_ref.shape
    rows = side // doms
    ids = centroid_iota(book_ref.shape[2], codes_ref.shape[2])
    for s in range(slots):
        codes = codes_ref[tl_ref[1, s] % plane].astype(F32)
        decode(codes, book_ref, ids, feats_ref)
        prod = contract(adj_ref[s], feats_ref[...].astype(BF16), 1, 1).astype(BF16)
        for j in range(doms):
            out_ref[j, s * rows : (s + 1) * rows, :] = prod[j * rows : (j + 1) * rows, :]
    out_ref[:, slots * rows :, :] = side_ref[...]


def node_kernel(
    got_ref, book_ref, wself_ref, wneigh_ref, bias_ref,
    send_ref, dpre_ref, agg_ref, feats_out, codes_out, feats_ref,
):
    doms, all_rows, width = got_ref.shape
    per = all_rows * 2 // 3
    rows = (all_rows - per) // 2
    group = 128 // per
    nodes = doms * rows
    subs = book_ref.shape[0]
    code_rows = got_ref[:, per + rows :, 0:128].reshape(nodes, 128)
    eye = (
        lax.broadcasted_iota(jnp.int32, (subs, 128), 0)
        == lax.broadcasted_iota(jnp.int32, (subs, 128), 1)
    ).astype(F32)
    codes = contract(eye.astype(BF16), code_rows, 1, 1)
    codes_out[...] = codes
    decode(codes, book_ref, centroid_iota(book_ref.shape[2], nodes), feats_ref)
    feats = feats_ref[...].astype(BF16)
    feats_out[...] = feats

    row_ids = lax.broadcasted_iota(jnp.int32, (nodes, 128), 0).astype(F32)
    picks = []
    total = jnp.zeros((nodes, width), F32)
    at = per + rows
    for g in range(doms // group):
        meta = got_ref[g * group, at : at + 1, 128:256].astype(F32)
        for b in range(1, group):
            meta = meta + got_ref[g * group + b, at : at + 1, 128:256].astype(F32)
        pick = jnp.where(row_ids == meta, 1.0, 0.0).astype(BF16)
        picks.append(pick)
        terms = got_ref[g * group : (g + 1) * group, 0:per, :].reshape(128, width)
        total = total + jnp.dot(pick, terms, preferred_element_type=F32)
    agg = total.astype(BF16)
    agg_ref[...] = agg
    pre = (
        contract(feats, wself_ref[...], 0, 0)
        + jnp.dot(agg, wneigh_ref[...], preferred_element_type=F32)
        + bias_ref[...]
    )
    gate = 1.0 / (1.0 + jnp.exp(-pre))
    hidden = pre * gate
    inv = lax.rsqrt(jnp.mean(hidden * hidden, axis=-1, keepdims=True) + 1e-05)
    send_ref[:, per:, :] = (hidden * inv).astype(BF16).reshape(doms, rows, width)
    cot = got_ref[:, per : per + rows, :].reshape(nodes, width).astype(F32)
    lean = jnp.mean(cot * hidden, axis=-1, keepdims=True) * (inv * inv * inv)
    dhidden = cot * inv - hidden * lean
    dpre = (dhidden * gate * (1.0 + pre * (1.0 - gate))).astype(BF16)
    dpre_ref[...] = dpre
    dagg = contract(dpre, wneigh_ref[...], 1, 1).astype(BF16)
    for g in range(doms // group):
        need = contract(picks[g], dagg, 0, 0).astype(BF16)
        send_ref[g * group : (g + 1) * group, 0:per, :] = need.reshape(group, per, width)


def weights_kernel(feats_ref, agg_ref, dpre_ref, w_ref, codes_ref, self_ref, neigh_ref, bias_ref, book_ref):
    dpre = dpre_ref[...]
    self_ref[...] = jnp.dot(feats_ref[...], dpre, preferred_element_type=F32)
    neigh_ref[...] = contract(agg_ref[...], dpre, 0, 0)
    bias = jnp.sum(dpre.astype(F32), axis=0, keepdims=True)
    bias_ref[...] = jnp.broadcast_to(bias, bias_ref.shape)
    dx = contract(w_ref[...], dpre, 1, 1)
    subs, sub_width, centroids = book_ref.shape
    ids = centroid_iota(centroids, codes_ref.shape[1])
    high = dx.astype(BF16)
    low = (dx - high.astype(F32)).astype(BF16)
    for m in range(subs):
        hot = onehot(codes_ref[m : m + 1, :], ids)
        at = slice(m * sub_width, (m + 1) * sub_width)
        book_ref[m] = contract(high[at], hot, 1, 1) + contract(low[at], hot, 1, 1)


def backward_kernel(
    tl_ref, got_ref, adj_ref, codes_ref, own_ref, self_ref, neigh_ref, bias_ref,
    keep_ref, give_ref, node_ref, dx_ref, book_ref,
):
    plane = codes_ref.shape[0]
    slots, side, _ = adj_ref.shape
    subs, sub_width, centroids = own_ref.shape
    doms, all_rows, width = got_ref.shape
    rows = side // doms
    per = slots * rows
    ids = centroid_iota(centroids, codes_ref.shape[2])
    book_ref[...] = own_ref[...]
    for s in range(slots):
        dagg = got_ref[:, s * rows : (s + 1) * rows, :].reshape(side, width)
        dx_ref[...] = contract(dagg, adj_ref[s], 0, 0).astype(BF16).astype(F32)
        codes = codes_ref[tl_ref[1, s] % plane].astype(F32)
        for m in range(subs):
            hot = onehot(codes[m : m + 1, :], ids)
            dx = dx_ref[m * sub_width : (m + 1) * sub_width, :].astype(BF16)
            book_ref[m] += contract(dx, hot, 1, 1)
    node_ref[...] = got_ref[:, per:, :].reshape(side, width)
    core = lax.axis_index("dom") % 2
    pieces = keep_ref.shape[0]
    half = width // pieces
    each = subs // pieces
    low = lax.broadcasted_iota(jnp.int32, (sub_width, centroids), 0) < sub_width // 2
    bias = bias_ref[...]

    def write(first_ref, second_ref):
        for j in range(pieces):
            first_ref[j, 0:half, :] = self_ref[j * half : (j + 1) * half, :]
            second_ref[j, 0:half, :] = neigh_ref[j * half : (j + 1) * half, :]
            for e in range(each):
                at = slice(half + e * sub_width, half + (e + 1) * sub_width)
                value = book_ref[j * each + e]
                first_ref[j, at, :] = jnp.where(low, value, bias)
                second_ref[j, at, :] = jnp.where(low, 0.0, value)

    @pl.when(core == 0)
    def _():
        write(keep_ref, give_ref)

    @pl.when(core == 1)
    def _():
        write(give_ref, keep_ref)


def pair_kernel(keep_ref, got_ref, out_ref):
    out_ref[...] = (keep_ref[...] + got_ref[...]).astype(out_ref.dtype)


def sum_spread_kernel(in_ref, out_ref):
    total = jnp.sum(in_ref[...].astype(F32), axis=0)
    out_ref[...] = jnp.broadcast_to(total[None].astype(out_ref.dtype), out_ref.shape)


def finish_kernel(mine_ref, other_ref, self_ref, neigh_ref, bias_ref, book_ref):
    core = lax.axis_index("dom") % 2
    pieces = mine_ref.shape[0]
    half = self_ref.shape[0] // pieces
    subs, sub_width, centroids = book_ref.shape
    each = subs // pieces
    low = lax.broadcasted_iota(jnp.int32, (sub_width, centroids), 0) < sub_width // 2

    def write(first_ref, second_ref):
        for j in range(pieces):
            first = first_ref[j].astype(F32)
            second = second_ref[j].astype(F32)
            self_ref[j * half : (j + 1) * half, :] = first[0:half]
            neigh_ref[j * half : (j + 1) * half, :] = second[0:half]
            for e in range(each):
                at = slice(half + e * sub_width, half + (e + 1) * sub_width)
                book_ref[j * each + e] = jnp.where(low, first[at], second[at])
        row = half + sub_width // 2
        bias_ref[...] = first_ref[0].astype(F32)[row : row + 1]

    @pl.when(core == 0)
    def _():
        write(mine_ref, other_ref)

    @pl.when(core == 1)
    def _():
        write(other_ref, mine_ref)


def exchange(x, axes, groups=None):
    return lax.all_to_all(x, axes, split_axis=0, concat_axis=0, tiled=True, axis_index_groups=groups)


def body(quantizer_codes, codebook, adj_tiles, tile_list, tile_count, w_self, w_neigh, out_bias, cotangent):
    doms = lax.axis_size("dom")
    plane = lax.axis_size("tile") * lax.axis_size("rep")
    subs, centroids, sub_width = codebook.shape
    slots, side = adj_tiles.shape[1:3]
    width = subs * sub_width
    rows = side // doms
    per = slots * rows
    codes = quantizer_codes.T
    book = codebook.transpose(0, 2, 1)
    adj = adj_tiles[0]
    slot_ids = tile_list[0].T
    bias = out_bias.reshape(1, width)
    swap = [(i, i ^ 1) for i in range(doms)]
    cores = [list(range(c, doms, 2)) for c in range(2)]

    spread = jnp.broadcast_to(codes.astype(BF16)[None], (plane, subs, side))
    all_codes = exchange(spread, PLANE)
    side_rows = call(
        functools.partial(side_kernel, plane), "side", struct((doms, 2 * rows, width), BF16),
        (slot_ids, tile_count), (codes, cotangent),
    )
    parts = call(
        forward_kernel, "forward", struct((doms, per + 2 * rows, width), BF16),
        (slot_ids,), (adj, all_codes, book, side_rows), (VM((width, side), F32),),
    )
    parts = exchange(parts, DOM)
    need, dpre, agg, feats, own_codes = call(
        node_kernel, "node",
        (struct((doms, per + rows, width), BF16), struct((side, width), BF16),
         struct((side, width), BF16), struct((width, side), BF16), struct((subs, side), F32)),
        (), (parts, book, w_self, w_neigh, bias), (VM((width, side), F32),),
    )
    need = exchange(need, DOM)
    grad_self, grad_neigh, grad_bias, own_book = call(
        weights_kernel, "weights",
        (struct((width, width), F32), struct((width, width), F32), struct((sub_width, width), F32),
         struct((subs, sub_width, centroids), F32)),
        (), (feats, agg, dpre, w_self, own_codes),
    )
    piece = (width + subs * sub_width) // plane
    keep, give, node_out = call(
        backward_kernel, "backward",
        (struct((plane, piece, width), F32), struct((plane, piece, width), F32), struct((side, width), BF16)),
        (slot_ids,), (need, adj, all_codes, own_book, grad_self, grad_neigh, grad_bias),
        (VM((width, side), F32), VM((subs, sub_width, centroids), F32)), 1,
    )
    got = lax.ppermute(give, "dom", swap)
    half = call(pair_kernel, "pair", struct((plane, piece, width), BF16), (), (keep, got))
    half = exchange(half, PLANE)
    half = call(sum_spread_kernel, "sum_plane", struct((doms // 2, piece, width), F32), (), (half,))
    half = exchange(half, "dom", cores)
    half = call(sum_spread_kernel, "sum_dom", struct((plane, piece, width), BF16), (), (half,))
    mine = exchange(half, PLANE)
    other = lax.ppermute(mine, "dom", swap)
    grad_self, grad_neigh, grad_bias, grad_book = call(
        finish_kernel, "finish",
        (struct((width, width), F32), struct((width, width), F32), struct((1, width), F32),
         struct((subs, sub_width, centroids), F32)),
        (), (mine, other), (), 4,
    )
    return (node_out, grad_self, grad_neigh, grad_bias.reshape(width), grad_book.transpose(0, 2, 1))


def solution(mesh):
    every = ("dom", "tile", "rep")
    in_specs = (
        P(every, None), P(), P(every, None, None, None), P(every, None, None), P(every),
        P(), P(), P(), P(every, None),
    )
    out_specs = (P(every, None), P(), P(), P(), P())
    return jax.shard_map(body, mesh=mesh, in_specs=in_specs, out_specs=out_specs, check_vma=False)
```

```python
import functools

import jax
import jax.numpy as jnp
from jax import lax
from jax.experimental import pallas as pl
from jax.experimental.pallas import tpu as pltpu
from jax.sharding import PartitionSpec as P

INTERPRET = False
F32 = jnp.float32
BF16 = jnp.bfloat16
VM = pltpu.VMEM
VMEM_LIMIT = 16 << 20
DOM = ("dom",)
PLANE = ("tile", "rep")


def contract(a, b, da, db):
    return lax.dot_general(a, b, (((da,), (db,)), ((), ())), preferred_element_type=F32)


def call(kernel, name, out_shape, scalars, arrays, scratch=(), final=0):
    if not INTERPRET:
        arrays = [pltpu.with_memory_space_constraint(a, VM) for a in arrays]
        shapes = out_shape if isinstance(out_shape, tuple) else (out_shape,)
        kept = len(shapes) - final
        shapes = tuple(VM(o.shape, o.dtype) if i < kept else o for i, o in enumerate(shapes))
        out_shape = shapes if isinstance(out_shape, tuple) else shapes[0]
    return pl.pallas_call(
        kernel,
        name=name,
        out_shape=out_shape,
        in_specs=[pl.BlockSpec(memory_space=pltpu.SMEM)] * len(scalars)
        + [pl.BlockSpec(memory_space=VM)] * len(arrays),
        out_specs=jax.tree.map(lambda _: pl.BlockSpec(memory_space=VM), out_shape),
        scratch_shapes=list(scratch),
        compiler_params=pltpu.CompilerParams(vmem_limit_bytes=VMEM_LIMIT),
        interpret=INTERPRET,
    )(*scalars, *arrays)


def struct(shape, dtype):
    return jax.ShapeDtypeStruct(shape, dtype)


def onehot(row, centroid_ids):
    return jnp.where(centroid_ids.astype(BF16) == row.astype(BF16), jnp.ones((), BF16), jnp.zeros((), BF16))


def centroid_iota(centroids, nodes):
    return lax.broadcasted_iota(jnp.int32, (centroids, nodes), 0).astype(F32)


def decode(codes, book_ref, ids, out_ref):
    sub_count, width, _ = book_ref.shape
    for m in range(sub_count):
        hot = onehot(codes[m : m + 1, :], ids)
        out_ref[m * width : (m + 1) * width, :] = jnp.dot(
            book_ref[m], hot, preferred_element_type=F32
        ).astype(out_ref.dtype)


def shifted_eye(count, shift):
    row = lax.broadcasted_iota(jnp.int32, (count, 128), 0)
    lane = lax.broadcasted_iota(jnp.int32, (count, 128), 1)
    return jnp.where(lane == row + shift, 1.0, 0.0).astype(BF16)


def spread_kernel(codes_ref, out_ref):
    out_ref[...] = jnp.broadcast_to(codes_ref[...].astype(F32).astype(BF16)[None], out_ref.shape)


def side_kernel(plane, tl_ref, tc_ref, codes_ref, cot_ref, bias_ref, side_ref, bias_out):
    doms, all_rows, width = side_ref.shape
    rows = all_rows * 2 // 3
    half = rows // 2
    subs, nodes = codes_ref.shape
    slots = tl_ref.shape[1]
    group = 128 // (slots * rows)
    codes = codes_ref[...].astype(F32).astype(BF16)
    first = contract(codes, shifted_eye(subs, 0), 0, 0)
    second = contract(codes, shifted_eye(subs, subs), 0, 0)
    at = lax.broadcasted_iota(jnp.int32, (half, 128), 1)
    at = at - (lax.axis_index("dom") % group) * (slots * rows)
    meta = jnp.zeros((half, 128), jnp.int32)
    for s in range(slots):
        target = tl_ref[0, s] // plane * rows
        here = (at >= s * rows) & (at < (s + 1) * rows)
        live = s < tc_ref[0]
        meta = jnp.where(here, jnp.where(live, target + at - s * rows, nodes), meta)
    meta = meta.astype(F32).astype(BF16)
    for j in range(doms):
        side_ref[j, 0:rows, :] = cot_ref[j * rows : (j + 1) * rows, :]
        pair = first[j * rows : j * rows + half] + second[j * rows + half : (j + 1) * rows]
        side_ref[j, rows:, 0:128] = pair.astype(BF16)
        side_ref[j, rows:, 128:256] = meta
    bias_out[...] = bias_ref[...]


def forward_kernel(tl_ref, adj_ref, codes_ref, book_ref, side_ref, out_ref, feats_ref):
    plane = codes_ref.shape[0]
    doms = out_ref.shape[0]
    slots, side, _ = adj_ref.shape
    rows = side // doms
    codes = jnp.concatenate([codes_ref[tl_ref[1, s] % plane].astype(F32) for s in range(slots)], axis=1)
    decode(codes, book_ref, centroid_iota(book_ref.shape[2], slots * side), feats_ref)
    for s in range(slots):
        feats = feats_ref[:, s * side : (s + 1) * side].astype(BF16)
        prod = contract(adj_ref[s], feats, 1, 1).astype(BF16)
        for j in range(doms):
            out_ref[j, s * rows : (s + 1) * rows, :] = prod[j * rows : (j + 1) * rows, :]
    out_ref[:, slots * rows :, :] = side_ref[...]


def node_kernel(
    slots, got_ref, book_ref, wself_ref, wneigh_ref, bias_ref,
    send_ref, dpre_ref, agg_ref, feats_out, codes_out, feats_ref,
):
    doms, all_rows, width = got_ref.shape
    rows = 2 * all_rows // (2 * slots + 3)
    half = rows // 2
    per = slots * rows
    group = 128 // per
    nodes = doms * rows
    subs = book_ref.shape[0]
    pairs = got_ref[:, per + rows :, 0:128].reshape(doms * half, 128)
    spot = lax.broadcasted_iota(jnp.int32, (doms * half, nodes), 0)
    spot = spot // half * rows + spot % half
    node = lax.broadcasted_iota(jnp.int32, (doms * half, nodes), 1)
    codes = jnp.zeros((subs, nodes), F32)
    for h in range(2):
        part = contract(shifted_eye(subs, h * subs), pairs, 1, 1).astype(BF16)
        place = jnp.where(node == spot + h * half, 1.0, 0.0).astype(BF16)
        codes = codes + jnp.dot(part, place, preferred_element_type=F32)
    codes_out[...] = codes
    decode(codes, book_ref, centroid_iota(book_ref.shape[2], nodes), feats_ref)
    feats = feats_ref[...].astype(BF16)
    feats_out[...] = feats

    row_ids = lax.broadcasted_iota(jnp.int32, (nodes, 128), 0).astype(F32)
    picks = []
    total = jnp.zeros((nodes, width), F32)
    at = per + rows
    for g in range(doms // group):
        meta = got_ref[g * group, at : at + 1, 128:256].astype(F32)
        for b in range(1, group):
            meta = meta + got_ref[g * group + b, at : at + 1, 128:256].astype(F32)
        pick = jnp.where(row_ids == meta, 1.0, 0.0).astype(BF16)
        picks.append(pick)
        terms = got_ref[g * group : (g + 1) * group, 0:per, :].reshape(128, width)
        total = total + jnp.dot(pick, terms, preferred_element_type=F32)
    agg = total.astype(BF16)
    agg_ref[...] = agg
    pre = (
        contract(feats, wself_ref[...], 0, 0)
        + jnp.dot(agg, wneigh_ref[...], preferred_element_type=F32)
        + bias_ref[...]
    )
    gate = 1.0 / (1.0 + jnp.exp(-pre))
    hidden = pre * gate
    inv = lax.rsqrt(jnp.mean(hidden * hidden, axis=-1, keepdims=True) + 1e-05)
    send_ref[:, per:, :] = (hidden * inv).astype(BF16).reshape(doms, rows, width)
    cot = got_ref[:, per : per + rows, :].reshape(nodes, width).astype(F32)
    lean = jnp.mean(cot * hidden, axis=-1, keepdims=True) * (inv * inv * inv)
    dhidden = cot * inv - hidden * lean
    dpre = (dhidden * gate * (1.0 + pre * (1.0 - gate))).astype(BF16)
    dpre_ref[...] = dpre
    dagg = contract(dpre, wneigh_ref[...], 1, 1).astype(BF16)
    for g in range(doms // group):
        need = contract(picks[g], dagg, 0, 0).astype(BF16)
        send_ref[g * group : (g + 1) * group, 0:per, :] = need.reshape(group, per, width)


def halves(write, keep_ref, give_ref):
    core = lax.axis_index("dom") % 2

    @pl.when(core == 0)
    def _():
        write(keep_ref, give_ref)

    @pl.when(core == 1)
    def _():
        write(give_ref, keep_ref)


def weights_kernel(feats_ref, agg_ref, dpre_ref, keep_ref, give_ref, bias_ref):
    dpre = dpre_ref[...]
    grad_self = jnp.dot(feats_ref[...], dpre, preferred_element_type=F32).reshape(keep_ref.shape)
    grad_neigh = contract(agg_ref[...], dpre, 0, 0).reshape(keep_ref.shape)
    bias = jnp.sum(dpre.astype(F32), axis=0, keepdims=True)
    bias_ref[...] = jnp.broadcast_to(bias, bias_ref.shape)

    def write(first_ref, second_ref):
        first_ref[...] = grad_self
        second_ref[...] = grad_neigh

    halves(write, keep_ref, give_ref)


def own_book_kernel(dpre_ref, w_ref, codes_ref, book_ref):
    dx = contract(w_ref[...], dpre_ref[...], 1, 1)
    subs, sub_width, centroids = book_ref.shape
    ids = centroid_iota(centroids, codes_ref.shape[1])
    high = dx.astype(BF16)
    low = (dx - high.astype(F32)).astype(BF16)
    for m in range(subs):
        hot = onehot(codes_ref[m : m + 1, :], ids)
        at = slice(m * sub_width, (m + 1) * sub_width)
        book_ref[m] = contract(high[at], hot, 1, 1) + contract(low[at], hot, 1, 1)


def backward_kernel(
    tl_ref, got_ref, adj_ref, codes_ref, own_ref, bias_ref,
    keep_ref, give_ref, node_ref, dx_ref, book_ref,
):
    plane = codes_ref.shape[0]
    slots, side, _ = adj_ref.shape
    subs, sub_width, centroids = own_ref.shape
    doms, all_rows, width = got_ref.shape
    rows = side // doms
    per = slots * rows
    ids = centroid_iota(centroids, slots * side)
    for s in range(slots):
        dagg = got_ref[:, s * rows : (s + 1) * rows, :].reshape(side, width)
        dx_ref[:, s * side : (s + 1) * side] = contract(dagg, adj_ref[s], 0, 0).astype(BF16).astype(F32)
    codes = jnp.concatenate([codes_ref[tl_ref[1, s] % plane].astype(F32) for s in range(slots)], axis=1)
    for m in range(subs):
        hot = onehot(codes[m : m + 1, :], ids)
        dx = dx_ref[m * sub_width : (m + 1) * sub_width, :].astype(BF16)
        book_ref[m] = own_ref[m] + contract(dx, hot, 1, 1)
    node_ref[...] = got_ref[:, per:, :].reshape(side, width)
    low = lax.broadcasted_iota(jnp.int32, (sub_width, centroids), 0) < sub_width // 2
    shape = keep_ref.shape

    def write(first_ref, second_ref):
        value = book_ref[...]
        first_ref[...] = jnp.where(low[None], value, bias_ref[...][None]).reshape(shape)
        second_ref[...] = jnp.where(low[None], 0.0, value).reshape(shape)

    halves(write, keep_ref, give_ref)


def pair_kernel(keep_ref, got_ref, keep_book_ref, got_book_ref, out_ref):
    half = keep_ref.shape[1]
    out_ref[:, 0:half, :] = (keep_ref[...] + got_ref[...]).astype(out_ref.dtype)
    out_ref[:, half:, :] = (keep_book_ref[...] + got_book_ref[...]).astype(out_ref.dtype)


def sum_spread_kernel(in_ref, out_ref):
    total = jnp.sum(in_ref[...].astype(F32), axis=0)
    out_ref[...] = jnp.broadcast_to(total[None].astype(out_ref.dtype), out_ref.shape)


def finish_kernel(mine_ref, other_ref, self_ref, neigh_ref, bias_ref, book_ref):
    core = lax.axis_index("dom") % 2
    pieces = mine_ref.shape[0]
    half = self_ref.shape[0] // pieces
    subs, sub_width, centroids = book_ref.shape
    each = subs // pieces
    low = lax.broadcasted_iota(jnp.int32, (sub_width, centroids), 0) < sub_width // 2

    def write(first_ref, second_ref):
        for j in range(pieces):
            first = first_ref[j].astype(F32)
            second = second_ref[j].astype(F32)
            self_ref[j * half : (j + 1) * half, :] = first[0:half]
            neigh_ref[j * half : (j + 1) * half, :] = second[0:half]
            for e in range(each):
                at = slice(half + e * sub_width, half + (e + 1) * sub_width)
                book_ref[j * each + e] = jnp.where(low, first[at], second[at])
        row = half + sub_width // 2
        bias_ref[...] = first_ref[0].astype(F32)[row : row + 1]

    @pl.when(core == 0)
    def _():
        write(mine_ref, other_ref)

    @pl.when(core == 1)
    def _():
        write(other_ref, mine_ref)


def exchange(x, axes, groups=None):
    return lax.all_to_all(x, axes, split_axis=0, concat_axis=0, tiled=True, axis_index_groups=groups)


def body(quantizer_codes, codebook, adj_tiles, tile_list, tile_count, w_self, w_neigh, out_bias, cotangent):
    doms = lax.axis_size("dom")
    plane = lax.axis_size("tile") * lax.axis_size("rep")
    subs, centroids, sub_width = codebook.shape
    slots, side = adj_tiles.shape[1:3]
    width = subs * sub_width
    rows = side // doms
    per = slots * rows
    codes = quantizer_codes.T
    book = codebook.transpose(0, 2, 1)
    adj = adj_tiles[0]
    slot_ids = tile_list[0].T
    swap = [(i, i ^ 1) for i in range(doms)]
    cores = [list(range(c, doms, 2)) for c in range(2)]

    spread = call(spread_kernel, "spread", struct((plane, subs, side), BF16), (), (codes,))
    all_codes = exchange(spread, PLANE)
    side_rows, bias = call(
        functools.partial(side_kernel, plane), "side",
        (struct((doms, rows + rows // 2, width), BF16), struct((1, width), F32)),
        (slot_ids, tile_count), (codes, cotangent, out_bias.reshape(1, width)),
    )
    parts = call(
        forward_kernel, "forward", struct((doms, per + rows + rows // 2, width), BF16),
        (slot_ids,), (adj, all_codes, book, side_rows), (VM((width, slots * side), F32),),
    )
    parts = exchange(parts, DOM)
    need, dpre, agg, feats, own_codes = call(
        functools.partial(node_kernel, slots), "node",
        (struct((doms, per + rows, width), BF16), struct((side, width), BF16),
         struct((side, width), BF16), struct((width, side), BF16), struct((subs, side), F32)),
        (), (parts, book, w_self, w_neigh, bias), (VM((width, side), F32),),
    )
    need = exchange(need, DOM)
    half = width // plane
    book_half = subs * sub_width // plane
    keep, give, grad_bias = call(
        weights_kernel, "weights",
        (struct((plane, half, width), F32), struct((plane, half, width), F32), struct((sub_width, width), F32)),
        (), (feats, agg, dpre),
    )
    got = lax.ppermute(give, "dom", swap)
    own_book = call(
        own_book_kernel, "own_book", struct((subs, sub_width, centroids), F32), (), (dpre, w_self, own_codes)
    )
    keep_book, give_book, node_out = call(
        backward_kernel, "backward",
        (struct((plane, book_half, width), F32), struct((plane, book_half, width), F32),
         struct((side, width), BF16)),
        (slot_ids,), (need, adj, all_codes, own_book, grad_bias),
        (VM((width, slots * side), F32), VM((subs, sub_width, centroids), F32)), 1,
    )
    got_book = lax.ppermute(give_book, "dom", swap)
    piece = half + book_half
    half = call(
        pair_kernel, "pair", struct((plane, piece, width), BF16), (), (keep, got, keep_book, got_book)
    )
    half = exchange(half, PLANE)
    half = call(sum_spread_kernel, "sum_plane", struct((doms // 2, piece, width), F32), (), (half,))
    half = exchange(half, "dom", cores)
    half = call(sum_spread_kernel, "sum_dom", struct((plane, piece, width), BF16), (), (half,))
    mine = exchange(half, PLANE)
    other = lax.ppermute(mine, "dom", swap)
    grad_self, grad_neigh, grad_bias, grad_book = call(
        finish_kernel, "finish",
        (struct((width, width), F32), struct((width, width), F32), struct((1, width), F32),
         struct((subs, sub_width, centroids), F32)),
        (), (mine, other), (), 4,
    )
    return (node_out, grad_self, grad_neigh, grad_bias.reshape(width), grad_book.transpose(0, 2, 1))


def solution(mesh):
    every = ("dom", "tile", "rep")
    in_specs = (
        P(every, None), P(), P(every, None, None, None), P(every, None, None), P(every),
        P(), P(), P(), P(every, None),
    )
    out_specs = (P(every, None), P(), P(), P(), P())
    return jax.shard_map(body, mesh=mesh, in_specs=in_specs, out_specs=out_specs, check_vma=False)
```

```python
import functools

import jax
import jax.numpy as jnp
from jax import lax
from jax.experimental import pallas as pl
from jax.experimental.pallas import tpu as pltpu
from jax.sharding import PartitionSpec as P

INTERPRET = False
F32 = jnp.float32
BF16 = jnp.bfloat16
VM = pltpu.VMEM
VMEM_LIMIT = 16 << 20
DOM = ("dom",)
PLANE = ("tile", "rep")


def contract(a, b, da, db):
    return lax.dot_general(a, b, (((da,), (db,)), ((), ())), preferred_element_type=F32)


def call(kernel, name, out_shape, scalars, arrays, scratch=(), final=0):
    if not INTERPRET:
        arrays = [pltpu.with_memory_space_constraint(a, VM) for a in arrays]
        shapes = out_shape if isinstance(out_shape, tuple) else (out_shape,)
        kept = len(shapes) - final
        shapes = tuple(VM(o.shape, o.dtype) if i < kept else o for i, o in enumerate(shapes))
        out_shape = shapes if isinstance(out_shape, tuple) else shapes[0]
    return pl.pallas_call(
        kernel,
        name=name,
        out_shape=out_shape,
        in_specs=[pl.BlockSpec(memory_space=pltpu.SMEM)] * len(scalars)
        + [pl.BlockSpec(memory_space=VM)] * len(arrays),
        out_specs=jax.tree.map(lambda _: pl.BlockSpec(memory_space=VM), out_shape),
        scratch_shapes=list(scratch),
        compiler_params=pltpu.CompilerParams(vmem_limit_bytes=VMEM_LIMIT),
        interpret=INTERPRET,
    )(*scalars, *arrays)


def struct(shape, dtype):
    return jax.ShapeDtypeStruct(shape, dtype)


def onehot(row, centroid_ids):
    return jnp.where(centroid_ids.astype(BF16) == row.astype(BF16), jnp.ones((), BF16), jnp.zeros((), BF16))


def centroid_iota(centroids, nodes):
    return lax.broadcasted_iota(jnp.int32, (centroids, nodes), 0).astype(F32)


def decode(codes, book_ref, ids, out_ref):
    sub_count, width, _ = book_ref.shape
    for m in range(sub_count):
        hot = onehot(codes[m : m + 1, :], ids)
        out_ref[m * width : (m + 1) * width, :] = jnp.dot(
            book_ref[m], hot, preferred_element_type=F32
        ).astype(out_ref.dtype)


def shifted_eye(count, shift):
    row = lax.broadcasted_iota(jnp.int32, (count, 128), 0)
    lane = lax.broadcasted_iota(jnp.int32, (count, 128), 1)
    return jnp.where(lane == row + shift, 1.0, 0.0).astype(BF16)


def spread_kernel(codes_ref, out_ref):
    out_ref[...] = jnp.broadcast_to(codes_ref[...].astype(F32).astype(BF16)[None], out_ref.shape)


def side_kernel(plane, tl_ref, tc_ref, codes_ref, cot_ref, bias_ref, side_ref, bias_out):
    doms, all_rows, width = side_ref.shape
    rows = all_rows * 2 // 3
    half = rows // 2
    subs, nodes = codes_ref.shape
    slots = tl_ref.shape[1]
    group = 128 // (slots * rows)
    codes = codes_ref[...].astype(F32).astype(BF16)
    first = contract(codes, shifted_eye(subs, 0), 0, 0)
    second = contract(codes, shifted_eye(subs, subs), 0, 0)
    at = lax.broadcasted_iota(jnp.int32, (half, 128), 1)
    at = at - (lax.axis_index("dom") % group) * (slots * rows)
    meta = jnp.zeros((half, 128), jnp.int32)
    for s in range(slots):
        target = tl_ref[0, s] // plane * rows
        here = (at >= s * rows) & (at < (s + 1) * rows)
        live = s < tc_ref[0]
        meta = jnp.where(here, jnp.where(live, target + at - s * rows, nodes), meta)
    meta = meta.astype(F32).astype(BF16)
    for j in range(doms):
        side_ref[j, 0:rows, :] = cot_ref[j * rows : (j + 1) * rows, :]
        pair = first[j * rows : j * rows + half] + second[j * rows + half : (j + 1) * rows]
        side_ref[j, rows:, 0:128] = pair.astype(BF16)
        side_ref[j, rows:, 128:256] = meta
    bias_out[...] = bias_ref[...]


def forward_kernel(tl_ref, adj_ref, codes_ref, book_ref, side_ref, out_ref, feats_ref):
    plane = codes_ref.shape[0]
    doms = out_ref.shape[0]
    slots, side, _ = adj_ref.shape
    rows = side // doms
    codes = jnp.concatenate([codes_ref[tl_ref[1, s] % plane].astype(F32) for s in range(slots)], axis=1)
    decode(codes, book_ref, centroid_iota(book_ref.shape[2], slots * side), feats_ref)
    for s in range(slots):
        feats = feats_ref[:, s * side : (s + 1) * side].astype(BF16)
        prod = contract(adj_ref[s], feats, 1, 1).astype(BF16)
        for j in range(doms):
            out_ref[j, s * rows : (s + 1) * rows, :] = prod[j * rows : (j + 1) * rows, :]
    out_ref[:, slots * rows :, :] = side_ref[...]


def node_kernel(
    slots, got_ref, book_ref, wself_ref, wneigh_ref, bias_ref,
    send_ref, dpre_ref, agg_ref, feats_out, codes_out, feats_ref,
):
    doms, all_rows, width = got_ref.shape
    rows = 2 * all_rows // (2 * slots + 3)
    half = rows // 2
    per = slots * rows
    group = 128 // per
    nodes = doms * rows
    subs = book_ref.shape[0]
    pairs = got_ref[:, per + rows :, 0:128].reshape(doms * half, 128)
    spot = lax.broadcasted_iota(jnp.int32, (doms * half, nodes), 0)
    spot = spot // half * rows + spot % half
    node = lax.broadcasted_iota(jnp.int32, (doms * half, nodes), 1)
    codes = jnp.zeros((subs, nodes), F32)
    for h in range(2):
        part = contract(shifted_eye(subs, h * subs), pairs, 1, 1).astype(BF16)
        place = jnp.where(node == spot + h * half, 1.0, 0.0).astype(BF16)
        codes = codes + jnp.dot(part, place, preferred_element_type=F32)
    codes_out[...] = codes
    decode(codes, book_ref, centroid_iota(book_ref.shape[2], nodes), feats_ref)
    feats = feats_ref[...].astype(BF16)
    feats_out[...] = feats

    row_ids = lax.broadcasted_iota(jnp.int32, (nodes, 128), 0).astype(F32)
    picks = []
    total = jnp.zeros((nodes, width), F32)
    at = per + rows
    for g in range(doms // group):
        meta = got_ref[g * group, at : at + 1, 128:256].astype(F32)
        for b in range(1, group):
            meta = meta + got_ref[g * group + b, at : at + 1, 128:256].astype(F32)
        pick = jnp.where(row_ids == meta, 1.0, 0.0).astype(BF16)
        picks.append(pick)
        terms = got_ref[g * group : (g + 1) * group, 0:per, :].reshape(128, width)
        total = total + jnp.dot(pick, terms, preferred_element_type=F32)
    agg = total.astype(BF16)
    agg_ref[...] = agg
    pre = (
        contract(feats, wself_ref[...], 0, 0)
        + jnp.dot(agg, wneigh_ref[...], preferred_element_type=F32)
        + bias_ref[...]
    )
    gate = 1.0 / (1.0 + jnp.exp(-pre))
    hidden = pre * gate
    inv = lax.rsqrt(jnp.mean(hidden * hidden, axis=-1, keepdims=True) + 1e-05)
    send_ref[:, per:, :] = (hidden * inv).astype(BF16).reshape(doms, rows, width)
    cot = got_ref[:, per : per + rows, :].reshape(nodes, width).astype(F32)
    lean = jnp.mean(cot * hidden, axis=-1, keepdims=True) * (inv * inv * inv)
    dhidden = cot * inv - hidden * lean
    dpre = (dhidden * gate * (1.0 + pre * (1.0 - gate))).astype(BF16)
    dpre_ref[...] = dpre
    dagg = contract(dpre, wneigh_ref[...], 1, 1).astype(BF16)
    for g in range(doms // group):
        need = contract(picks[g], dagg, 0, 0).astype(BF16)
        send_ref[g * group : (g + 1) * group, 0:per, :] = need.reshape(group, per, width)


def halves(write, keep_ref, give_ref):
    core = lax.axis_index("dom") % 2

    @pl.when(core == 0)
    def _():
        write(keep_ref, give_ref)

    @pl.when(core == 1)
    def _():
        write(give_ref, keep_ref)


def weights_kernel(feats_ref, agg_ref, dpre_ref, keep_ref, give_ref, bias_ref):
    dpre = dpre_ref[...]
    grad_self = jnp.dot(feats_ref[...], dpre, preferred_element_type=F32).reshape(keep_ref.shape)
    grad_neigh = contract(agg_ref[...], dpre, 0, 0).reshape(keep_ref.shape)
    bias = jnp.sum(dpre.astype(F32), axis=0, keepdims=True)
    bias_ref[...] = jnp.broadcast_to(bias, bias_ref.shape)

    def write(first_ref, second_ref):
        first_ref[...] = grad_self
        second_ref[...] = grad_neigh

    halves(write, keep_ref, give_ref)


def own_book_kernel(dpre_ref, w_ref, codes_ref, book_ref):
    dx = contract(w_ref[...], dpre_ref[...], 1, 1)
    subs, sub_width, centroids = book_ref.shape
    ids = centroid_iota(centroids, codes_ref.shape[1])
    high = dx.astype(BF16)
    low = (dx - high.astype(F32)).astype(BF16)
    for m in range(subs):
        hot = onehot(codes_ref[m : m + 1, :], ids)
        at = slice(m * sub_width, (m + 1) * sub_width)
        book_ref[m] = contract(high[at], hot, 1, 1) + contract(low[at], hot, 1, 1)


def backward_kernel(
    tl_ref, got_ref, adj_ref, codes_ref, own_ref, keep_ref, pair_ref, bias_ref, out_ref, node_ref, dx_ref
):
    slots, side, _ = adj_ref.shape
    subs, sub_width, centroids = own_ref.shape
    doms, all_rows, width = got_ref.shape
    rows = side // doms
    per = slots * rows
    for s in range(slots):
        dagg = got_ref[:, s * rows : (s + 1) * rows, :].reshape(side, width)
        dx_ref[:, s * side : (s + 1) * side] = contract(dagg, adj_ref[s], 0, 0).astype(BF16).astype(F32)
    pieces, half, _ = keep_ref.shape
    each = subs // pieces
    low = lax.broadcasted_iota(jnp.int32, (8, 128), 0) < 4
    bias = bias_ref[...]
    bias = jnp.where(low, bias[:, 0:128], bias[:, 128:256]).astype(out_ref.dtype)
    plane = codes_ref.shape[0]
    ids = centroid_iota(centroids, slots * side)
    codes = jnp.concatenate([codes_ref[tl_ref[1, s] % plane].astype(F32) for s in range(slots)], axis=1)
    grads = keep_ref[...] + pair_ref[...]
    for h in range(2):
        lanes = slice(h * 128, (h + 1) * 128)
        out_ref[:, h * half : (h + 1) * half, :] = grads[:, :, lanes].astype(out_ref.dtype)
    base = 2 * half
    tail = base + 2 * each * sub_width
    out_ref[:, tail:, :] = jnp.broadcast_to(bias[None], (pieces, 8, 128))
    for m in range(subs):
        hot = onehot(codes[m : m + 1, :], ids)
        dx = dx_ref[m * sub_width : (m + 1) * sub_width, :].astype(BF16)
        value = own_ref[m] + contract(dx, hot, 1, 1)
        for h in range(2):
            at = base + (2 * (m % each) + h) * sub_width
            out_ref[m // each, at : at + sub_width, :] = value[:, h * 128 : (h + 1) * 128].astype(out_ref.dtype)
    node_ref[...] = got_ref[:, per:, :].reshape(side, width)


def plane_sum_kernel(in_ref, out_ref):
    total = jnp.sum(in_ref[...].astype(F32), axis=0)
    out_ref[...] = jnp.broadcast_to(total[None].astype(out_ref.dtype), out_ref.shape)


def dom_sum_kernel(half, in_ref, out_ref, bias_ref):
    doms, rows, _ = in_ref.shape
    even = jnp.zeros((rows, 128), F32)
    odd = jnp.zeros((rows, 128), F32)
    for d in range(0, doms, 2):
        even = even + in_ref[d].astype(F32)
        odd = odd + in_ref[d + 1].astype(F32)
    both = even + odd
    blocks = [even[0 : 2 * half], odd[0 : 2 * half]]
    count = (rows - 8 - 2 * half) // 16
    blocks += [both[2 * half + 16 * e : 2 * half + 16 * (e + 1)] for e in range(count)]
    at = 0
    for block in blocks:
        tall = block.shape[0] // 2
        for h in range(2):
            value = block[h * tall : (h + 1) * tall].astype(out_ref.dtype)
            out_ref[:, at : at + tall, h * 128 : (h + 1) * 128] = jnp.broadcast_to(
                value[None], (out_ref.shape[0], tall, 128)
            )
        at += tall
    bias_ref[:, 0:128] = both[rows - 8 : rows - 7]
    bias_ref[:, 128:256] = both[rows - 1 : rows]


def finish_kernel(in_ref, bias_ref, self_ref, neigh_ref, bias_out, book_ref):
    pieces = in_ref.shape[0]
    half = self_ref.shape[0] // pieces
    self_ref[...] = in_ref[:, 0:half, :].astype(F32).reshape(self_ref.shape)
    neigh_ref[...] = in_ref[:, half : 2 * half, :].astype(F32).reshape(neigh_ref.shape)
    book_ref[...] = in_ref[:, 2 * half :, :].astype(F32).reshape(book_ref.shape)
    bias_out[...] = bias_ref[...]


def exchange(x, axes):
    return lax.all_to_all(x, axes, split_axis=0, concat_axis=0, tiled=True)


def body(quantizer_codes, codebook, adj_tiles, tile_list, tile_count, w_self, w_neigh, out_bias, cotangent):
    doms = lax.axis_size("dom")
    plane = lax.axis_size("tile") * lax.axis_size("rep")
    subs, centroids, sub_width = codebook.shape
    slots, side = adj_tiles.shape[1:3]
    width = subs * sub_width
    rows = side // doms
    per = slots * rows
    codes = quantizer_codes.T
    book = codebook.transpose(0, 2, 1)
    adj = adj_tiles[0]
    slot_ids = tile_list[0].T
    swap = [(i, i ^ 1) for i in range(doms)]

    spread = call(spread_kernel, "spread", struct((plane, subs, side), BF16), (), (codes,))
    all_codes = exchange(spread, PLANE)
    side_rows, bias = call(
        functools.partial(side_kernel, plane), "side",
        (struct((doms, rows + rows // 2, width), BF16), struct((1, width), F32)),
        (slot_ids, tile_count), (codes, cotangent, out_bias.reshape(1, width)),
    )
    parts = call(
        forward_kernel, "forward", struct((doms, per + rows + rows // 2, width), BF16),
        (slot_ids,), (adj, all_codes, book, side_rows), (VM((width, slots * side), F32),),
    )
    parts = exchange(parts, DOM)
    need, dpre, agg, feats, own_codes = call(
        functools.partial(node_kernel, slots), "node",
        (struct((doms, per + rows, width), BF16), struct((side, width), BF16),
         struct((side, width), BF16), struct((width, side), BF16), struct((subs, side), F32)),
        (), (parts, book, w_self, w_neigh, bias), (VM((width, side), F32),),
    )
    need = exchange(need, DOM)
    half = width // plane
    book_half = subs * sub_width // plane
    keep, give, grad_bias = call(
        weights_kernel, "weights",
        (struct((plane, half, width), F32), struct((plane, half, width), F32), struct((sub_width, width), F32)),
        (), (feats, agg, dpre),
    )
    got = lax.ppermute(give, "dom", swap)
    own_book = call(
        own_book_kernel, "own_book", struct((subs, sub_width, centroids), F32), (), (dpre, w_self, own_codes)
    )
    piece = 2 * half + 2 * book_half + 8
    part, node_out = call(
        backward_kernel, "backward",
        (struct((plane, piece, 128), BF16), struct((side, width), BF16)),
        (slot_ids,), (need, adj, all_codes, own_book, keep, got, grad_bias),
        (VM((width, slots * side), F32),), 1,
    )
    part = exchange(part, PLANE)
    part = call(plane_sum_kernel, "plane_sum", struct((doms, piece, 128), BF16), (), (part,))
    part = exchange(part, DOM)
    part, grad_bias = call(
        functools.partial(dom_sum_kernel, half), "dom_sum",
        (struct((plane, 2 * half + book_half, width), BF16), struct((1, width), F32)), (), (part,),
    )
    part = exchange(part, PLANE)
    grad_self, grad_neigh, grad_bias, grad_book = call(
        finish_kernel, "finish",
        (struct((width, width), F32), struct((width, width), F32), struct((1, width), F32),
         struct((subs, sub_width, centroids), F32)),
        (), (part, grad_bias), (), 4,
    )
    return (node_out, grad_self, grad_neigh, grad_bias.reshape(width), grad_book.transpose(0, 2, 1))


def solution(mesh):
    every = ("dom", "tile", "rep")
    in_specs = (
        P(every, None), P(), P(every, None, None, None), P(every, None, None), P(every),
        P(), P(), P(), P(every, None),
    )
    out_specs = (P(every, None), P(), P(), P(), P())
    return jax.shard_map(body, mesh=mesh, in_specs=in_specs, out_specs=out_specs, check_vma=False)
```

```python
import functools

import jax
import jax.numpy as jnp
from jax import lax
from jax.experimental import pallas as pl
from jax.experimental.pallas import tpu as pltpu
from jax.sharding import PartitionSpec as P

INTERPRET = False
F32 = jnp.float32
BF16 = jnp.bfloat16
VM = pltpu.VMEM
VMEM_LIMIT = 16 << 20
DOM = ("dom",)
PLANE = ("tile", "rep")


def contract(a, b, da, db):
    return lax.dot_general(a, b, (((da,), (db,)), ((), ())), preferred_element_type=F32)


def call(kernel, name, out_shape, scalars, arrays, scratch=(), final=0, pin=True):
    if not INTERPRET:
        arrays = [pltpu.with_memory_space_constraint(a, VM if pin else pltpu.HBM) for a in arrays]
        shapes = out_shape if isinstance(out_shape, tuple) else (out_shape,)
        kept = len(shapes) - final
        shapes = tuple(VM(o.shape, o.dtype) if i < kept else o for i, o in enumerate(shapes))
        out_shape = shapes if isinstance(out_shape, tuple) else shapes[0]
    return pl.pallas_call(
        kernel,
        name=name,
        out_shape=out_shape,
        in_specs=[pl.BlockSpec(memory_space=pltpu.SMEM)] * len(scalars)
        + [pl.BlockSpec(memory_space=VM)] * len(arrays),
        out_specs=jax.tree.map(lambda _: pl.BlockSpec(memory_space=VM), out_shape),
        scratch_shapes=list(scratch),
        compiler_params=pltpu.CompilerParams(vmem_limit_bytes=VMEM_LIMIT),
        interpret=INTERPRET,
    )(*scalars, *arrays)


def struct(shape, dtype):
    return jax.ShapeDtypeStruct(shape, dtype)


def onehot(row, centroid_ids):
    return jnp.where(centroid_ids.astype(BF16) == row.astype(BF16), jnp.ones((), BF16), jnp.zeros((), BF16))


def centroid_iota(centroids, nodes):
    return lax.broadcasted_iota(jnp.int32, (centroids, nodes), 0).astype(F32)


def decode(codes, book_ref, ids, out_ref):
    sub_count, width, _ = book_ref.shape
    for m in range(sub_count):
        hot = onehot(codes[m : m + 1, :], ids)
        out_ref[m * width : (m + 1) * width, :] = jnp.dot(
            book_ref[m], hot, preferred_element_type=F32
        ).astype(out_ref.dtype)


def shifted_eye(count, shift):
    row = lax.broadcasted_iota(jnp.int32, (count, 128), 0)
    lane = lax.broadcasted_iota(jnp.int32, (count, 128), 1)
    return jnp.where(lane == row + shift, 1.0, 0.0).astype(BF16)


def spread_kernel(codes_ref, out_ref):
    out_ref[...] = jnp.broadcast_to(codes_ref[...].astype(F32).astype(BF16)[None], out_ref.shape)


def side_kernel(plane, tl_ref, tc_ref, codes_ref, cot_ref, bias_ref, side_ref, bias_out):
    doms, all_rows, width = side_ref.shape
    rows = all_rows * 2 // 3
    half = rows // 2
    subs, nodes = codes_ref.shape
    slots = tl_ref.shape[1]
    group = 128 // (slots * rows)
    codes = codes_ref[...].astype(F32).astype(BF16)
    first = contract(codes, shifted_eye(subs, 0), 0, 0)
    second = contract(codes, shifted_eye(subs, subs), 0, 0)
    at = lax.broadcasted_iota(jnp.int32, (half, 128), 1)
    at = at - (lax.axis_index("dom") % group) * (slots * rows)
    meta = jnp.zeros((half, 128), jnp.int32)
    for s in range(slots):
        target = tl_ref[0, s] // plane * rows
        here = (at >= s * rows) & (at < (s + 1) * rows)
        live = s < tc_ref[0]
        meta = jnp.where(here, jnp.where(live, target + at - s * rows, nodes), meta)
    meta = meta.astype(F32).astype(BF16)
    for j in range(doms):
        side_ref[j, 0:rows, :] = cot_ref[j * rows : (j + 1) * rows, :]
        pair = first[j * rows : j * rows + half] + second[j * rows + half : (j + 1) * rows]
        side_ref[j, rows:, 0:128] = pair.astype(BF16)
        side_ref[j, rows:, 128:256] = meta
    bias_out[...] = bias_ref[...]


def forward_kernel(tl_ref, adj_ref, codes_ref, book_ref, side_ref, out_ref, feats_ref):
    plane = codes_ref.shape[0]
    doms = out_ref.shape[0]
    slots, side, _ = adj_ref.shape
    rows = side // doms
    codes = jnp.concatenate([codes_ref[tl_ref[1, s] % plane].astype(F32) for s in range(slots)], axis=1)
    decode(codes, book_ref, centroid_iota(book_ref.shape[2], slots * side), feats_ref)
    for s in range(slots):
        feats = feats_ref[:, s * side : (s + 1) * side].astype(BF16)
        prod = contract(adj_ref[s], feats, 1, 1).astype(BF16)
        for j in range(doms):
            out_ref[j, s * rows : (s + 1) * rows, :] = prod[j * rows : (j + 1) * rows, :]
    out_ref[:, slots * rows :, :] = side_ref[...]


def node_kernel(
    slots, got_ref, book_ref, wself_ref, wneigh_ref, bias_ref,
    send_ref, dpre_ref, agg_ref, feats_out, codes_out, feats_ref,
):
    doms, all_rows, width = got_ref.shape
    rows = 2 * all_rows // (2 * slots + 3)
    half = rows // 2
    per = slots * rows
    group = 128 // per
    nodes = doms * rows
    subs = book_ref.shape[0]
    pairs = got_ref[:, per + rows :, 0:128].reshape(doms * half, 128)
    spot = lax.broadcasted_iota(jnp.int32, (doms * half, nodes), 0)
    spot = spot // half * rows + spot % half
    node = lax.broadcasted_iota(jnp.int32, (doms * half, nodes), 1)
    codes = jnp.zeros((subs, nodes), F32)
    for h in range(2):
        part = contract(shifted_eye(subs, h * subs), pairs, 1, 1).astype(BF16)
        place = jnp.where(node == spot + h * half, 1.0, 0.0).astype(BF16)
        codes = codes + jnp.dot(part, place, preferred_element_type=F32)
    codes_out[...] = codes
    decode(codes, book_ref, centroid_iota(book_ref.shape[2], nodes), feats_ref)
    feats = feats_ref[...].astype(BF16)
    feats_out[...] = feats

    row_ids = lax.broadcasted_iota(jnp.int32, (nodes, 128), 0).astype(F32)
    picks = []
    total = jnp.zeros((nodes, width), F32)
    at = per + rows
    for g in range(doms // group):
        meta = got_ref[g * group, at : at + 1, 128:256].astype(F32)
        for b in range(1, group):
            meta = meta + got_ref[g * group + b, at : at + 1, 128:256].astype(F32)
        pick = jnp.where(row_ids == meta, 1.0, 0.0).astype(BF16)
        picks.append(pick)
        terms = got_ref[g * group : (g + 1) * group, 0:per, :].reshape(128, width)
        total = total + jnp.dot(pick, terms, preferred_element_type=F32)
    agg = total.astype(BF16)
    agg_ref[...] = agg
    pre = (
        contract(feats, wself_ref[...], 0, 0)
        + jnp.dot(agg, wneigh_ref[...], preferred_element_type=F32)
        + bias_ref[...]
    )
    gate = 1.0 / (1.0 + jnp.exp(-pre))
    hidden = pre * gate
    inv = lax.rsqrt(jnp.mean(hidden * hidden, axis=-1, keepdims=True) + 1e-05)
    send_ref[:, per:, :] = (hidden * inv).astype(BF16).reshape(doms, rows, width)
    cot = got_ref[:, per : per + rows, :].reshape(nodes, width).astype(F32)
    lean = jnp.mean(cot * hidden, axis=-1, keepdims=True) * (inv * inv * inv)
    dhidden = cot * inv - hidden * lean
    dpre = (dhidden * gate * (1.0 + pre * (1.0 - gate))).astype(BF16)
    dpre_ref[...] = dpre
    dagg = contract(dpre, wneigh_ref[...], 1, 1).astype(BF16)
    for g in range(doms // group):
        need = contract(picks[g], dagg, 0, 0).astype(BF16)
        send_ref[g * group : (g + 1) * group, 0:per, :] = need.reshape(group, per, width)


def halves(write, keep_ref, give_ref):
    core = lax.axis_index("dom") % 2

    @pl.when(core == 0)
    def _():
        write(keep_ref, give_ref)

    @pl.when(core == 1)
    def _():
        write(give_ref, keep_ref)


def weights_kernel(feats_ref, agg_ref, dpre_ref, keep_ref, give_ref, bias_ref):
    dpre = dpre_ref[...]
    grad_self = jnp.dot(feats_ref[...], dpre, preferred_element_type=F32).reshape(keep_ref.shape)
    grad_neigh = contract(agg_ref[...], dpre, 0, 0).reshape(keep_ref.shape)
    bias = jnp.sum(dpre.astype(F32), axis=0, keepdims=True)
    bias_ref[...] = jnp.broadcast_to(bias, bias_ref.shape)

    def write(first_ref, second_ref):
        first_ref[...] = grad_self
        second_ref[...] = grad_neigh

    halves(write, keep_ref, give_ref)


def own_book_kernel(dpre_ref, w_ref, codes_ref, book_ref):
    dx = contract(w_ref[...], dpre_ref[...], 1, 1)
    subs, sub_width, centroids = book_ref.shape
    ids = centroid_iota(centroids, codes_ref.shape[1])
    high = dx.astype(BF16)
    low = (dx - high.astype(F32)).astype(BF16)
    for m in range(subs):
        hot = onehot(codes_ref[m : m + 1, :], ids)
        at = slice(m * sub_width, (m + 1) * sub_width)
        book_ref[m] = contract(high[at], hot, 1, 1) + contract(low[at], hot, 1, 1)


def backward_kernel(
    tl_ref, got_ref, adj_ref, codes_ref, own_ref, grads_ref, out_ref, node_ref, dx_ref
):
    slots, side, _ = adj_ref.shape
    subs, sub_width, centroids = own_ref.shape
    doms, all_rows, width = got_ref.shape
    rows = side // doms
    per = slots * rows
    for s in range(slots):
        dagg = got_ref[:, s * rows : (s + 1) * rows, :].reshape(side, width)
        dx_ref[:, s * side : (s + 1) * side] = contract(dagg, adj_ref[s], 0, 0).astype(BF16).astype(F32)
    pieces, base, _ = grads_ref.shape
    base = base - 8
    each = subs // pieces
    out_ref[:, 0:base, :] = grads_ref[:, 0:base, :]
    out_ref[:, base + 2 * each * sub_width :, :] = grads_ref[:, base:, :]
    plane = codes_ref.shape[0]
    ids = centroid_iota(centroids, slots * side)
    codes = jnp.concatenate([codes_ref[tl_ref[1, s] % plane].astype(F32) for s in range(slots)], axis=1)
    for m in range(subs):
        hot = onehot(codes[m : m + 1, :], ids)
        dx = dx_ref[m * sub_width : (m + 1) * sub_width, :].astype(BF16)
        value = own_ref[m] + contract(dx, hot, 1, 1)
        for h in range(2):
            at = base + (2 * (m % each) + h) * sub_width
            out_ref[m // each, at : at + sub_width, :] = value[:, h * 128 : (h + 1) * 128].astype(out_ref.dtype)
    node_ref[...] = got_ref[:, per:, :].reshape(side, width)


def pair_kernel(keep_ref, got_ref, bias_ref, out_ref):
    pieces, half, _ = keep_ref.shape
    grads = keep_ref[...] + got_ref[...]
    for h in range(2):
        lanes = slice(h * 128, (h + 1) * 128)
        out_ref[:, h * half : (h + 1) * half, :] = grads[:, :, lanes].astype(out_ref.dtype)
    low = lax.broadcasted_iota(jnp.int32, (8, 128), 0) < 4
    bias = bias_ref[...]
    bias = jnp.where(low, bias[:, 0:128], bias[:, 128:256]).astype(out_ref.dtype)
    out_ref[:, 2 * half :, :] = jnp.broadcast_to(bias[None], (pieces, 8, 128))


def plane_sum_kernel(in_ref, out_ref):
    total = jnp.sum(in_ref[...].astype(F32), axis=0)
    out_ref[...] = jnp.broadcast_to(total[None].astype(out_ref.dtype), out_ref.shape)


def dom_sum_kernel(half, in_ref, out_ref, bias_ref):
    doms, rows, _ = in_ref.shape
    even = jnp.zeros((rows, 128), F32)
    odd = jnp.zeros((rows, 128), F32)
    for d in range(0, doms, 2):
        even = even + in_ref[d].astype(F32)
        odd = odd + in_ref[d + 1].astype(F32)
    both = even + odd
    blocks = [even[0 : 2 * half], odd[0 : 2 * half]]
    count = (rows - 8 - 2 * half) // 16
    blocks += [both[2 * half + 16 * e : 2 * half + 16 * (e + 1)] for e in range(count)]
    first = lax.axis_index("dom") % 2 == 0
    at = 0
    for block in blocks:
        tall = block.shape[0] // 2
        value = jnp.where(first, block[0:tall], block[tall:]).astype(out_ref.dtype)
        out_ref[:, at : at + tall, :] = jnp.broadcast_to(value[None], (out_ref.shape[0], tall, 128))
        at += tall
    bias_ref[:, 0:128] = both[rows - 8 : rows - 7]
    bias_ref[:, 128:256] = both[rows - 1 : rows]


def finish_kernel(mine_ref, other_ref, bias_ref, self_ref, neigh_ref, bias_out, book_ref):
    pieces = mine_ref.shape[0]
    half = self_ref.shape[0] // pieces
    first = lax.axis_index("dom") % 2 == 0
    for h in range(2):
        lanes = slice(h * 128, (h + 1) * 128)
        mine, other = mine_ref[...].astype(F32), other_ref[...].astype(F32)
        value = jnp.where(first, mine, other) if h == 0 else jnp.where(first, other, mine)
        self_ref[:, lanes] = value[:, 0:half].reshape(self_ref.shape[0], 128)
        neigh_ref[:, lanes] = value[:, half : 2 * half].reshape(self_ref.shape[0], 128)
        book_ref[:, :, lanes] = value[:, 2 * half :].reshape(book_ref.shape[0], book_ref.shape[1], 128)
    bias_out[...] = bias_ref[...]


def exchange(x, axes):
    return lax.all_to_all(x, axes, split_axis=0, concat_axis=0, tiled=True)


def body(quantizer_codes, codebook, adj_tiles, tile_list, tile_count, w_self, w_neigh, out_bias, cotangent):
    doms = lax.axis_size("dom")
    plane = lax.axis_size("tile") * lax.axis_size("rep")
    subs, centroids, sub_width = codebook.shape
    slots, side = adj_tiles.shape[1:3]
    width = subs * sub_width
    rows = side // doms
    per = slots * rows
    codes = quantizer_codes.T
    book = codebook.transpose(0, 2, 1)
    adj = adj_tiles[0]
    slot_ids = tile_list[0].T
    swap = [(i, i ^ 1) for i in range(doms)]

    spread = call(spread_kernel, "spread", struct((plane, subs, side), BF16), (), (codes,), pin=False)
    all_codes = exchange(spread, PLANE)
    side_rows, bias = call(
        functools.partial(side_kernel, plane), "side",
        (struct((doms, rows + rows // 2, width), BF16), struct((1, width), F32)),
        (slot_ids, tile_count), (codes, cotangent, out_bias.reshape(1, width)),
    )
    parts = call(
        forward_kernel, "forward", struct((doms, per + rows + rows // 2, width), BF16),
        (slot_ids,), (adj, all_codes, book, side_rows), (VM((width, slots * side), F32),),
    )
    parts = exchange(parts, DOM)
    need, dpre, agg, feats, own_codes = call(
        functools.partial(node_kernel, slots), "node",
        (struct((doms, per + rows, width), BF16), struct((side, width), BF16),
         struct((side, width), BF16), struct((width, side), BF16), struct((subs, side), F32)),
        (), (parts, book, w_self, w_neigh, bias), (VM((width, side), F32),),
    )
    need = exchange(need, DOM)
    half = width // plane
    book_half = subs * sub_width // plane
    keep, give, grad_bias = call(
        weights_kernel, "weights",
        (struct((plane, half, width), F32), struct((plane, half, width), F32), struct((sub_width, width), F32)),
        (), (feats, agg, dpre),
    )
    got = lax.ppermute(give, "dom", swap)
    grads = call(
        pair_kernel, "pair", struct((plane, 2 * half + 8, 128), BF16), (), (keep, got, grad_bias)
    )
    own_book = call(
        own_book_kernel, "own_book", struct((subs, sub_width, centroids), F32), (), (dpre, w_self, own_codes)
    )
    piece = 2 * half + 2 * book_half + 8
    part, node_out = call(
        backward_kernel, "backward",
        (struct((plane, piece, 128), BF16), struct((side, width), BF16)),
        (slot_ids,), (need, adj, all_codes, own_book, grads),
        (VM((width, slots * side), F32),), 1,
    )
    part = exchange(part, PLANE)
    part = call(plane_sum_kernel, "plane_sum", struct((doms, piece, 128), BF16), (), (part,))
    part = exchange(part, DOM)
    part, grad_bias = call(
        functools.partial(dom_sum_kernel, half), "dom_sum",
        (struct((plane, 2 * half + book_half, 128), BF16), struct((1, width), F32)), (), (part,),
    )
    part = exchange(part, PLANE)
    grad_self, grad_neigh, grad_bias, grad_book = call(
        finish_kernel, "finish",
        (struct((width, width), F32), struct((width, width), F32), struct((1, width), F32),
         struct((subs, sub_width, centroids), F32)),
        (), (part, lax.ppermute(part, "dom", swap), grad_bias), (), 4,
    )
    return (node_out, grad_self, grad_neigh, grad_bias.reshape(width), grad_book.transpose(0, 2, 1))


def solution(mesh):
    every = ("dom", "tile", "rep")
    in_specs = (
        P(every, None), P(), P(every, None, None, None), P(every, None, None), P(every),
        P(), P(), P(), P(every, None),
    )
    out_specs = (P(every, None), P(), P(), P(), P())
    return jax.shard_map(body, mesh=mesh, in_specs=in_specs, out_specs=out_specs, check_vma=False)
```

```python
import functools

import jax
import jax.numpy as jnp
from jax import lax
from jax.experimental import pallas as pl
from jax.experimental.pallas import tpu as pltpu
from jax.sharding import PartitionSpec as P

INTERPRET = False
F32 = jnp.float32
BF16 = jnp.bfloat16
VM = pltpu.VMEM
VMEM_LIMIT = 16 << 20
DOM = ("dom",)
PLANE = ("tile", "rep")


def contract(a, b, da, db):
    return lax.dot_general(a, b, (((da,), (db,)), ((), ())), preferred_element_type=F32)


def call(kernel, name, out_shape, scalars, arrays, scratch=(), final=0, pin=True):
    if not INTERPRET:
        arrays = [pltpu.with_memory_space_constraint(a, VM if pin else pltpu.HBM) for a in arrays]
        shapes = out_shape if isinstance(out_shape, tuple) else (out_shape,)
        kept = len(shapes) - final
        shapes = tuple(VM(o.shape, o.dtype) if i < kept else o for i, o in enumerate(shapes))
        out_shape = shapes if isinstance(out_shape, tuple) else shapes[0]
    return pl.pallas_call(
        kernel,
        name=name,
        out_shape=out_shape,
        in_specs=[pl.BlockSpec(memory_space=pltpu.SMEM)] * len(scalars)
        + [pl.BlockSpec(memory_space=VM)] * len(arrays),
        out_specs=jax.tree.map(lambda _: pl.BlockSpec(memory_space=VM), out_shape),
        scratch_shapes=list(scratch),
        compiler_params=pltpu.CompilerParams(vmem_limit_bytes=VMEM_LIMIT),
        interpret=INTERPRET,
    )(*scalars, *arrays)


def struct(shape, dtype):
    return jax.ShapeDtypeStruct(shape, dtype)


def onehot(row, centroid_ids):
    return jnp.where(centroid_ids.astype(BF16) == row.astype(BF16), jnp.ones((), BF16), jnp.zeros((), BF16))


def centroid_iota(centroids, nodes):
    return lax.broadcasted_iota(jnp.int32, (centroids, nodes), 0).astype(F32)


def decode(codes, book_ref, ids, out_ref):
    sub_count, width, _ = book_ref.shape
    for m in range(sub_count):
        hot = onehot(codes[m : m + 1, :], ids)
        out_ref[m * width : (m + 1) * width, :] = jnp.dot(
            book_ref[m], hot, preferred_element_type=F32
        ).astype(out_ref.dtype)


def shifted_eye(count, shift):
    row = lax.broadcasted_iota(jnp.int32, (count, 128), 0)
    lane = lax.broadcasted_iota(jnp.int32, (count, 128), 1)
    return jnp.where(lane == row + shift, 1.0, 0.0).astype(BF16)


def spread_kernel(codes_ref, out_ref):
    out_ref[...] = jnp.broadcast_to(codes_ref[...].astype(F32).astype(BF16)[None], out_ref.shape)


def side_kernel(plane, tl_ref, tc_ref, codes_ref, cot_ref, bias_ref, side_ref, bias_out):
    doms, all_rows, width = side_ref.shape
    rows = all_rows * 2 // 3
    half = rows // 2
    subs, nodes = codes_ref.shape
    slots = tl_ref.shape[1]
    group = 128 // (slots * rows)
    codes = codes_ref[...].astype(F32).astype(BF16)
    first = contract(codes, shifted_eye(subs, 0), 0, 0)
    second = contract(codes, shifted_eye(subs, subs), 0, 0)
    at = lax.broadcasted_iota(jnp.int32, (half, 128), 1)
    at = at - (lax.axis_index("dom") % group) * (slots * rows)
    meta = jnp.zeros((half, 128), jnp.int32)
    for s in range(slots):
        target = tl_ref[0, s] // plane * rows
        here = (at >= s * rows) & (at < (s + 1) * rows)
        live = s < tc_ref[0]
        meta = jnp.where(here, jnp.where(live, target + at - s * rows, nodes), meta)
    meta = meta.astype(F32).astype(BF16)
    for j in range(doms):
        side_ref[j, 0:rows, :] = cot_ref[j * rows : (j + 1) * rows, :]
        pair = first[j * rows : j * rows + half] + second[j * rows + half : (j + 1) * rows]
        side_ref[j, rows:, 0:128] = pair.astype(BF16)
        side_ref[j, rows:, 128:256] = meta
    bias_out[...] = bias_ref[...]


def forward_kernel(tl_ref, adj_ref, codes_ref, book_ref, side_ref, out_ref, feats_ref):
    plane = codes_ref.shape[0]
    doms = out_ref.shape[0]
    slots, side, _ = adj_ref.shape
    rows = side // doms
    codes = jnp.concatenate([codes_ref[tl_ref[1, s] % plane].astype(F32) for s in range(slots)], axis=1)
    decode(codes, book_ref, centroid_iota(book_ref.shape[2], slots * side), feats_ref)
    for s in range(slots):
        feats = feats_ref[:, s * side : (s + 1) * side].astype(BF16)
        prod = contract(adj_ref[s], feats, 1, 1).astype(BF16)
        for j in range(doms):
            out_ref[j, s * rows : (s + 1) * rows, :] = prod[j * rows : (j + 1) * rows, :]
    out_ref[:, slots * rows :, :] = side_ref[...]


def node_kernel(
    slots, got_ref, book_ref, wself_ref, wneigh_ref, bias_ref,
    send_ref, dpre_ref, agg_ref, feats_out, codes_out, feats_ref,
):
    doms, all_rows, width = got_ref.shape
    rows = 2 * all_rows // (2 * slots + 3)
    half = rows // 2
    per = slots * rows
    group = 128 // per
    nodes = doms * rows
    subs = book_ref.shape[0]
    pairs = got_ref[:, per + rows :, 0:128].reshape(doms * half, 128)
    spot = lax.broadcasted_iota(jnp.int32, (doms * half, nodes), 0)
    spot = spot // half * rows + spot % half
    node = lax.broadcasted_iota(jnp.int32, (doms * half, nodes), 1)
    codes = jnp.zeros((subs, nodes), F32)
    for h in range(2):
        part = contract(shifted_eye(subs, h * subs), pairs, 1, 1).astype(BF16)
        place = jnp.where(node == spot + h * half, 1.0, 0.0).astype(BF16)
        codes = codes + jnp.dot(part, place, preferred_element_type=F32)
    codes_out[...] = codes
    decode(codes, book_ref, centroid_iota(book_ref.shape[2], nodes), feats_ref)
    feats = feats_ref[...].astype(BF16)
    feats_out[...] = feats

    row_ids = lax.broadcasted_iota(jnp.int32, (nodes, 128), 0).astype(F32)
    picks = []
    total = jnp.zeros((nodes, width), F32)
    at = per + rows
    for g in range(doms // group):
        meta = got_ref[g * group, at : at + 1, 128:256].astype(F32)
        for b in range(1, group):
            meta = meta + got_ref[g * group + b, at : at + 1, 128:256].astype(F32)
        pick = jnp.where(row_ids == meta, 1.0, 0.0).astype(BF16)
        picks.append(pick)
        terms = got_ref[g * group : (g + 1) * group, 0:per, :].reshape(128, width)
        total = total + jnp.dot(pick, terms, preferred_element_type=F32)
    agg = total.astype(BF16)
    agg_ref[...] = agg
    pre = (
        contract(feats, wself_ref[...], 0, 0)
        + jnp.dot(agg, wneigh_ref[...], preferred_element_type=F32)
        + bias_ref[...]
    )
    gate = 1.0 / (1.0 + jnp.exp(-pre))
    hidden = pre * gate
    inv = lax.rsqrt(jnp.mean(hidden * hidden, axis=-1, keepdims=True) + 1e-05)
    send_ref[:, per:, :] = (hidden * inv).astype(BF16).reshape(doms, rows, width)
    cot = got_ref[:, per : per + rows, :].reshape(nodes, width).astype(F32)
    lean = jnp.mean(cot * hidden, axis=-1, keepdims=True) * (inv * inv * inv)
    dhidden = cot * inv - hidden * lean
    dpre = (dhidden * gate * (1.0 + pre * (1.0 - gate))).astype(BF16)
    dpre_ref[...] = dpre
    dagg = contract(dpre, wneigh_ref[...], 1, 1).astype(BF16)
    for g in range(doms // group):
        need = contract(picks[g], dagg, 0, 0).astype(BF16)
        send_ref[g * group : (g + 1) * group, 0:per, :] = need.reshape(group, per, width)


def halves(write, keep_ref, give_ref):
    core = lax.axis_index("dom") % 2

    @pl.when(core == 0)
    def _():
        write(keep_ref, give_ref)

    @pl.when(core == 1)
    def _():
        write(give_ref, keep_ref)


def weights_kernel(feats_ref, agg_ref, dpre_ref, keep_ref, give_ref):
    dpre = dpre_ref[...]
    pieces, half, width = keep_ref.shape
    pieces = pieces - 1
    grad_self = jnp.dot(feats_ref[...], dpre, preferred_element_type=F32).reshape(pieces, half, width)
    grad_neigh = contract(agg_ref[...], dpre, 0, 0).reshape(pieces, half, width)
    bias = jnp.sum(dpre.astype(F32), axis=0, keepdims=True)
    keep_ref[pieces] = jnp.broadcast_to(bias, (half, width))
    give_ref[pieces] = jnp.broadcast_to(bias, (half, width))

    def write(first_ref, second_ref):
        first_ref[0:pieces] = grad_self
        second_ref[0:pieces] = grad_neigh

    halves(write, keep_ref, give_ref)


def own_book_kernel(dpre_ref, w_ref, codes_ref, book_ref):
    dx = contract(w_ref[...], dpre_ref[...], 1, 1)
    subs, sub_width, centroids = book_ref.shape
    ids = centroid_iota(centroids, codes_ref.shape[1])
    high = dx.astype(BF16)
    low = (dx - high.astype(F32)).astype(BF16)
    for m in range(subs):
        hot = onehot(codes_ref[m : m + 1, :], ids)
        at = slice(m * sub_width, (m + 1) * sub_width)
        book_ref[m] = contract(high[at], hot, 1, 1) + contract(low[at], hot, 1, 1)


def backward_kernel(
    tl_ref, got_ref, adj_ref, codes_ref, own_ref, grads_ref, out_ref, node_ref, dx_ref
):
    slots, side, _ = adj_ref.shape
    subs, sub_width, centroids = own_ref.shape
    doms, all_rows, width = got_ref.shape
    rows = side // doms
    per = slots * rows
    for s in range(slots):
        dagg = got_ref[:, s * rows : (s + 1) * rows, :].reshape(side, width)
        dx_ref[:, s * side : (s + 1) * side] = contract(dagg, adj_ref[s], 0, 0).astype(BF16).astype(F32)
    pieces, base, _ = grads_ref.shape
    base = base - 8
    each = subs // pieces
    out_ref[:, 0:base, :] = grads_ref[:, 0:base, :]
    out_ref[:, base + 2 * each * sub_width :, :] = grads_ref[:, base:, :]
    plane = codes_ref.shape[0]
    ids = centroid_iota(centroids, slots * side)
    codes = jnp.concatenate([codes_ref[tl_ref[1, s] % plane].astype(F32) for s in range(slots)], axis=1)
    for m in range(subs):
        hot = onehot(codes[m : m + 1, :], ids)
        dx = dx_ref[m * sub_width : (m + 1) * sub_width, :].astype(BF16)
        value = own_ref[m] + contract(dx, hot, 1, 1)
        for h in range(2):
            at = base + (2 * (m % each) + h) * sub_width
            out_ref[m // each, at : at + sub_width, :] = value[:, h * 128 : (h + 1) * 128].astype(out_ref.dtype)
    node_ref[...] = got_ref[:, per:, :].reshape(side, width)


def pair_kernel(keep_ref, got_ref, out_ref):
    pieces = out_ref.shape[0]
    half = keep_ref.shape[1]
    grads = keep_ref[0:pieces] + got_ref[0:pieces]
    for h in range(2):
        lanes = slice(h * 128, (h + 1) * 128)
        out_ref[:, h * half : (h + 1) * half, :] = grads[:, :, lanes].astype(out_ref.dtype)
    low = lax.broadcasted_iota(jnp.int32, (8, 128), 0) < 4
    bias = keep_ref[pieces, 0:8, :] + got_ref[pieces, 0:8, :]
    bias = jnp.where(low, bias[:, 0:128], bias[:, 128:256]).astype(out_ref.dtype)
    out_ref[:, 2 * half :, :] = jnp.broadcast_to(bias[None], (pieces, 8, 128))


def plane_sum_kernel(in_ref, out_ref):
    total = jnp.sum(in_ref[...].astype(F32), axis=0)
    out_ref[...] = jnp.broadcast_to(total[None].astype(out_ref.dtype), out_ref.shape)


def z_sum_kernel(in_ref, out_ref, bias_ref):
    total = jnp.sum(in_ref[...], axis=0)
    rows = out_ref.shape[1]
    out_ref[...] = jnp.broadcast_to(total[None, 0:rows].astype(out_ref.dtype), out_ref.shape)
    bias_ref[...] = total[rows:]


def finish_kernel(mine_ref, other_ref, bias_ref, self_ref, neigh_ref, bias_out, book_ref):
    pieces = mine_ref.shape[0]
    half = self_ref.shape[0] // pieces
    subs, sub_width, _ = book_ref.shape
    each = subs // pieces
    first = lax.axis_index("dom") % 2 == 0
    mine, other = mine_ref[...].astype(F32), other_ref[...].astype(F32)
    bias = bias_ref[...]
    for h in range(2):
        lanes = slice(h * 128, (h + 1) * 128)
        at = slice(h * half, (h + 1) * half)
        self_ref[:, lanes] = jnp.where(first, mine[:, at], other[:, at]).reshape(self_ref.shape[0], 128)
        neigh_ref[:, lanes] = jnp.where(first, other[:, at], mine[:, at]).reshape(self_ref.shape[0], 128)
        for e in range(each):
            start = 2 * half + (2 * e + h) * sub_width
            book = mine[:, start : start + sub_width] + other[:, start : start + sub_width]
            for j in range(pieces):
                book_ref[j * each + e, :, lanes] = book[j]
        bias_out[:, lanes] = bias[7 * h : 7 * h + 1]


def exchange(x, axes, groups=None):
    return lax.all_to_all(x, axes, split_axis=0, concat_axis=0, tiled=True, axis_index_groups=groups)


def body(quantizer_codes, codebook, adj_tiles, tile_list, tile_count, w_self, w_neigh, out_bias, cotangent):
    doms = lax.axis_size("dom")
    plane = lax.axis_size("tile") * lax.axis_size("rep")
    subs, centroids, sub_width = codebook.shape
    slots, side = adj_tiles.shape[1:3]
    width = subs * sub_width
    rows = side // doms
    per = slots * rows
    codes = quantizer_codes.T
    book = codebook.transpose(0, 2, 1)
    adj = adj_tiles[0]
    slot_ids = tile_list[0].T
    swap = [(i, i ^ 1) for i in range(doms)]
    cores = [list(range(c, doms, 2)) for c in range(2)]

    spread = call(spread_kernel, "spread", struct((plane, subs, side), BF16), (), (codes,), pin=False)
    all_codes = exchange(spread, PLANE)
    side_rows, bias = call(
        functools.partial(side_kernel, plane), "side",
        (struct((doms, rows + rows // 2, width), BF16), struct((1, width), F32)),
        (slot_ids, tile_count), (codes, cotangent, out_bias.reshape(1, width)),
    )
    parts = call(
        forward_kernel, "forward", struct((doms, per + rows + rows // 2, width), BF16),
        (slot_ids,), (adj, all_codes, book, side_rows), (VM((width, slots * side), F32),),
    )
    parts = exchange(parts, DOM)
    need, dpre, agg, feats, own_codes = call(
        functools.partial(node_kernel, slots), "node",
        (struct((doms, per + rows, width), BF16), struct((side, width), BF16),
         struct((side, width), BF16), struct((width, side), BF16), struct((subs, side), F32)),
        (), (parts, book, w_self, w_neigh, bias), (VM((width, side), F32),),
    )
    need = exchange(need, DOM)
    half = width // plane
    book_half = subs * sub_width // plane
    keep, give = call(
        weights_kernel, "weights",
        (struct((plane + 1, half, width), F32), struct((plane + 1, half, width), F32)), (), (feats, agg, dpre),
    )
    got = lax.ppermute(give, "dom", swap)
    grads = call(
        pair_kernel, "pair", struct((plane, 2 * half + 8, 128), BF16), (), (keep, got)
    )
    own_book = call(
        own_book_kernel, "own_book", struct((subs, sub_width, centroids), F32), (), (dpre, w_self, own_codes)
    )
    piece = 2 * half + 2 * book_half + 8
    part, node_out = call(
        backward_kernel, "backward",
        (struct((plane, piece, 128), BF16), struct((side, width), BF16)),
        (slot_ids,), (need, adj, all_codes, own_book, grads),
        (VM((width, slots * side), F32),), 1,
    )
    part = exchange(part, PLANE)
    part = call(plane_sum_kernel, "plane_sum", struct((doms // 2, piece, 128), F32), (), (part,))
    part = exchange(part, "dom", cores)
    part, grad_bias = call(
        z_sum_kernel, "z_sum", (struct((plane, piece - 8, 128), BF16), struct((8, 128), F32)), (), (part,)
    )
    part = exchange(part, PLANE)
    grad_self, grad_neigh, grad_bias, grad_book = call(
        finish_kernel, "finish",
        (struct((width, width), F32), struct((width, width), F32), struct((1, width), F32),
         struct((subs, sub_width, centroids), F32)),
        (), (part, lax.ppermute(part, "dom", swap), grad_bias), (), 4,
    )
    return (node_out, grad_self, grad_neigh, grad_bias.reshape(width), grad_book.transpose(0, 2, 1))


def solution(mesh):
    every = ("dom", "tile", "rep")
    in_specs = (
        P(every, None), P(), P(every, None, None, None), P(every, None, None), P(every),
        P(), P(), P(), P(every, None),
    )
    out_specs = (P(every, None), P(), P(), P(), P())
    return jax.shard_map(body, mesh=mesh, in_specs=in_specs, out_specs=out_specs, check_vma=False)
```

```python
import functools

import jax
import jax.numpy as jnp
from jax import lax
from jax.experimental import pallas as pl
from jax.experimental.pallas import tpu as pltpu
from jax.sharding import PartitionSpec as P

INTERPRET = False
F32 = jnp.float32
BF16 = jnp.bfloat16
VM = pltpu.VMEM
VMEM_LIMIT = 16 << 20
DOM = ("dom",)
PLANE = ("tile", "rep")


def contract(a, b, da, db):
    return lax.dot_general(a, b, (((da,), (db,)), ((), ())), preferred_element_type=F32)


def call(kernel, name, out_shape, scalars, arrays, scratch=(), final=0, pin=True):
    if not INTERPRET:
        arrays = [pltpu.with_memory_space_constraint(a, VM if pin else pltpu.HBM) for a in arrays]
        shapes = out_shape if isinstance(out_shape, tuple) else (out_shape,)
        kept = len(shapes) - final
        shapes = tuple(VM(o.shape, o.dtype) if i < kept else o for i, o in enumerate(shapes))
        out_shape = shapes if isinstance(out_shape, tuple) else shapes[0]
    return pl.pallas_call(
        kernel,
        name=name,
        out_shape=out_shape,
        in_specs=[pl.BlockSpec(memory_space=pltpu.SMEM)] * len(scalars)
        + [pl.BlockSpec(memory_space=VM)] * len(arrays),
        out_specs=jax.tree.map(lambda _: pl.BlockSpec(memory_space=VM), out_shape),
        scratch_shapes=list(scratch),
        compiler_params=pltpu.CompilerParams(vmem_limit_bytes=VMEM_LIMIT),
        interpret=INTERPRET,
    )(*scalars, *arrays)


def struct(shape, dtype):
    return jax.ShapeDtypeStruct(shape, dtype)


def onehot(row, centroid_ids):
    return jnp.where(centroid_ids.astype(BF16) == row.astype(BF16), jnp.ones((), BF16), jnp.zeros((), BF16))


def centroid_iota(centroids, nodes):
    return lax.broadcasted_iota(jnp.int32, (centroids, nodes), 0).astype(F32)


def decode(codes, book_ref, ids, out_ref):
    sub_count, width, _ = book_ref.shape
    for m in range(sub_count):
        hot = onehot(codes[m : m + 1, :], ids)
        out_ref[m * width : (m + 1) * width, :] = jnp.dot(
            book_ref[m], hot, preferred_element_type=F32
        ).astype(out_ref.dtype)


def shifted_eye(count, shift):
    row = lax.broadcasted_iota(jnp.int32, (count, 128), 0)
    lane = lax.broadcasted_iota(jnp.int32, (count, 128), 1)
    return jnp.where(lane == row + shift, 1.0, 0.0).astype(BF16)


def spread_kernel(codes_ref, out_ref):
    out_ref[...] = jnp.broadcast_to(codes_ref[...].astype(F32).astype(BF16)[None], out_ref.shape)


def side_kernel(plane, tl_ref, tc_ref, codes_ref, cot_ref, bias_ref, side_ref, bias_out):
    doms, all_rows, width = side_ref.shape
    rows = all_rows * 2 // 3
    half = rows // 2
    subs, nodes = codes_ref.shape
    slots = tl_ref.shape[1]
    group = 128 // (slots * rows)
    codes = codes_ref[...].astype(F32).astype(BF16)
    first = contract(codes, shifted_eye(subs, 0), 0, 0)
    second = contract(codes, shifted_eye(subs, subs), 0, 0)
    at = lax.broadcasted_iota(jnp.int32, (half, 128), 1)
    at = at - (lax.axis_index("dom") % group) * (slots * rows)
    meta = jnp.zeros((half, 128), jnp.int32)
    for s in range(slots):
        target = tl_ref[0, s] // plane * rows
        here = (at >= s * rows) & (at < (s + 1) * rows)
        live = s < tc_ref[0]
        meta = jnp.where(here, jnp.where(live, target + at - s * rows, nodes), meta)
    meta = meta.astype(F32).astype(BF16)
    for j in range(doms):
        side_ref[j, 0:rows, :] = cot_ref[j * rows : (j + 1) * rows, :]
        pair = first[j * rows : j * rows + half] + second[j * rows + half : (j + 1) * rows]
        side_ref[j, rows:, 0:128] = pair.astype(BF16)
        side_ref[j, rows:, 128:256] = meta
    bias_out[...] = bias_ref[...]


def forward_kernel(tl_ref, adj_ref, codes_ref, book_ref, side_ref, out_ref, feats_ref):
    plane = codes_ref.shape[0]
    doms = out_ref.shape[0]
    slots, side, _ = adj_ref.shape
    rows = side // doms
    codes = jnp.concatenate([codes_ref[tl_ref[1, s] % plane].astype(F32) for s in range(slots)], axis=1)
    decode(codes, book_ref, centroid_iota(book_ref.shape[2], slots * side), feats_ref)
    for s in range(slots):
        feats = feats_ref[:, s * side : (s + 1) * side].astype(BF16)
        prod = contract(adj_ref[s], feats, 1, 1).astype(BF16)
        for j in range(doms):
            out_ref[j, s * rows : (s + 1) * rows, :] = prod[j * rows : (j + 1) * rows, :]
    out_ref[:, slots * rows :, :] = side_ref[...]


def node_kernel(
    slots, got_ref, book_ref, wself_ref, wneigh_ref, bias_ref,
    send_ref, dpre_ref, agg_ref, feats_out, codes_out, feats_ref,
):
    doms, all_rows, width = got_ref.shape
    rows = 2 * all_rows // (2 * slots + 3)
    half = rows // 2
    per = slots * rows
    group = 128 // per
    nodes = doms * rows
    subs = book_ref.shape[0]
    pairs = got_ref[:, per + rows :, 0:128].reshape(doms * half, 128)
    spot = lax.broadcasted_iota(jnp.int32, (doms * half, nodes), 0)
    spot = spot // half * rows + spot % half
    node = lax.broadcasted_iota(jnp.int32, (doms * half, nodes), 1)
    codes = jnp.zeros((subs, nodes), F32)
    for h in range(2):
        part = contract(shifted_eye(subs, h * subs), pairs, 1, 1).astype(BF16)
        place = jnp.where(node == spot + h * half, 1.0, 0.0).astype(BF16)
        codes = codes + jnp.dot(part, place, preferred_element_type=F32)
    codes_out[...] = codes
    decode(codes, book_ref, centroid_iota(book_ref.shape[2], nodes), feats_ref)
    feats = feats_ref[...].astype(BF16)
    feats_out[...] = feats

    row_ids = lax.broadcasted_iota(jnp.int32, (nodes, 128), 0).astype(F32)
    picks = []
    total = jnp.zeros((nodes, width), F32)
    at = per + rows
    for g in range(doms // group):
        meta = got_ref[g * group, at : at + 1, 128:256].astype(F32)
        for b in range(1, group):
            meta = meta + got_ref[g * group + b, at : at + 1, 128:256].astype(F32)
        pick = jnp.where(row_ids == meta, 1.0, 0.0).astype(BF16)
        picks.append(pick)
        terms = got_ref[g * group : (g + 1) * group, 0:per, :].reshape(128, width)
        total = total + jnp.dot(pick, terms, preferred_element_type=F32)
    agg = total.astype(BF16)
    agg_ref[...] = agg
    pre = (
        contract(feats, wself_ref[...], 0, 0)
        + jnp.dot(agg, wneigh_ref[...], preferred_element_type=F32)
        + bias_ref[...]
    )
    gate = 1.0 / (1.0 + jnp.exp(-pre))
    hidden = pre * gate
    inv = lax.rsqrt(jnp.mean(hidden * hidden, axis=-1, keepdims=True) + 1e-05)
    send_ref[:, per:, :] = (hidden * inv).astype(BF16).reshape(doms, rows, width)
    cot = got_ref[:, per : per + rows, :].reshape(nodes, width).astype(F32)
    lean = jnp.mean(cot * hidden, axis=-1, keepdims=True) * (inv * inv * inv)
    dhidden = cot * inv - hidden * lean
    dpre = (dhidden * gate * (1.0 + pre * (1.0 - gate))).astype(BF16)
    dpre_ref[...] = dpre
    dagg = contract(dpre, wneigh_ref[...], 1, 1).astype(BF16)
    for g in range(doms // group):
        need = contract(picks[g], dagg, 0, 0).astype(BF16)
        send_ref[g * group : (g + 1) * group, 0:per, :] = need.reshape(group, per, width)


def halves(write, keep_ref, give_ref):
    core = lax.axis_index("dom") % 2

    @pl.when(core == 0)
    def _():
        write(keep_ref, give_ref)

    @pl.when(core == 1)
    def _():
        write(give_ref, keep_ref)


def weights_kernel(feats_ref, agg_ref, dpre_ref, keep_ref, give_ref):
    dpre = dpre_ref[...]
    pieces, half, width = keep_ref.shape
    pieces = pieces - 1
    grad_self = jnp.dot(feats_ref[...], dpre, preferred_element_type=F32).reshape(pieces, half, width)
    grad_neigh = contract(agg_ref[...], dpre, 0, 0).reshape(pieces, half, width)
    bias = jnp.sum(dpre.astype(F32), axis=0, keepdims=True)
    keep_ref[pieces] = jnp.broadcast_to(bias, (half, width))
    give_ref[pieces] = jnp.broadcast_to(bias, (half, width))

    def write(first_ref, second_ref):
        first_ref[0:pieces] = grad_self
        second_ref[0:pieces] = grad_neigh

    halves(write, keep_ref, give_ref)


def own_book_kernel(dpre_ref, w_ref, codes_ref, book_ref):
    dx = contract(w_ref[...], dpre_ref[...], 1, 1)
    subs, sub_width, centroids = book_ref.shape
    ids = centroid_iota(centroids, codes_ref.shape[1])
    high = dx.astype(BF16)
    low = (dx - high.astype(F32)).astype(BF16)
    for m in range(subs):
        hot = onehot(codes_ref[m : m + 1, :], ids)
        at = slice(m * sub_width, (m + 1) * sub_width)
        book_ref[m] = contract(high[at], hot, 1, 1) + contract(low[at], hot, 1, 1)


def backward_kernel(
    tl_ref, got_ref, adj_ref, codes_ref, own_ref, grads_ref, out_ref, node_ref, dx_ref
):
    slots, side, _ = adj_ref.shape
    subs, sub_width, centroids = own_ref.shape
    doms, all_rows, width = got_ref.shape
    rows = side // doms
    per = slots * rows
    for s in range(slots):
        dagg = got_ref[:, s * rows : (s + 1) * rows, :].reshape(side, width)
        dx_ref[:, s * side : (s + 1) * side] = contract(dagg, adj_ref[s], 0, 0).astype(BF16).astype(F32)
    pieces, base, _ = grads_ref.shape
    base = base - 8
    each = subs // pieces
    out_ref[:, 0:base, :] = grads_ref[:, 0:base, :]
    out_ref[:, base + 2 * each * sub_width :, :] = grads_ref[:, base:, :]
    plane = codes_ref.shape[0]
    ids = centroid_iota(centroids, slots * side)
    codes = jnp.concatenate([codes_ref[tl_ref[1, s] % plane].astype(F32) for s in range(slots)], axis=1)
    for m in range(subs):
        hot = onehot(codes[m : m + 1, :], ids)
        dx = dx_ref[m * sub_width : (m + 1) * sub_width, :].astype(BF16)
        value = own_ref[m] + contract(dx, hot, 1, 1)
        for h in range(2):
            at = base + (2 * (m % each) + h) * sub_width
            out_ref[m // each, at : at + sub_width, :] = value[:, h * 128 : (h + 1) * 128].astype(out_ref.dtype)
    node_ref[...] = got_ref[:, per:, :].reshape(side, width)


def pair_kernel(keep_ref, got_ref, out_ref):
    pieces = out_ref.shape[0]
    half = keep_ref.shape[1]
    grads = keep_ref[0:pieces] + got_ref[0:pieces]
    for h in range(2):
        lanes = slice(h * 128, (h + 1) * 128)
        out_ref[:, h * half : (h + 1) * half, :] = grads[:, :, lanes].astype(out_ref.dtype)
    low = lax.broadcasted_iota(jnp.int32, (8, 128), 0) < 4
    bias = keep_ref[pieces, 0:8, :] + got_ref[pieces, 0:8, :]
    bias = jnp.where(low, bias[:, 0:128], bias[:, 128:256]).astype(out_ref.dtype)
    out_ref[:, 2 * half :, :] = jnp.broadcast_to(bias[None], (pieces, 8, 128))


def plane_sum_kernel(in_ref, out_ref):
    total = jnp.sum(in_ref[...].astype(F32), axis=0)
    spare = jnp.zeros((out_ref.shape[1] - total.shape[0], total.shape[1]), F32)
    total = jnp.concatenate([total, spare], axis=0).astype(out_ref.dtype)
    out_ref[...] = jnp.broadcast_to(total[None], out_ref.shape)


def z_sum_kernel(in_ref, out_ref, bias_ref):
    total = jnp.sum(in_ref[...].astype(F32), axis=0)
    rows = out_ref.shape[1]
    out_ref[...] = jnp.broadcast_to(total[None, 0:rows].astype(out_ref.dtype), out_ref.shape)
    bias_ref[...] = total[rows : rows + 8]


def finish_kernel(mine_ref, other_ref, bias_ref, self_ref, neigh_ref, bias_out, book_ref):
    pieces = mine_ref.shape[0]
    half = self_ref.shape[0] // pieces
    subs, sub_width, _ = book_ref.shape
    each = subs // pieces
    first = lax.axis_index("dom") % 2 == 0
    mine, other = mine_ref[...].astype(F32), other_ref[...].astype(F32)
    bias = bias_ref[...]
    for h in range(2):
        lanes = slice(h * 128, (h + 1) * 128)
        at = slice(h * half, (h + 1) * half)
        self_ref[:, lanes] = jnp.where(first, mine[:, at], other[:, at]).reshape(self_ref.shape[0], 128)
        neigh_ref[:, lanes] = jnp.where(first, other[:, at], mine[:, at]).reshape(self_ref.shape[0], 128)
        for e in range(each):
            start = 2 * half + (2 * e + h) * sub_width
            book = mine[:, start : start + sub_width] + other[:, start : start + sub_width]
            for j in range(pieces):
                book_ref[j * each + e, :, lanes] = book[j]
        bias_out[:, lanes] = bias[7 * h : 7 * h + 1]


def exchange(x, axes, groups=None):
    return lax.all_to_all(x, axes, split_axis=0, concat_axis=0, tiled=True, axis_index_groups=groups)


def body(quantizer_codes, codebook, adj_tiles, tile_list, tile_count, w_self, w_neigh, out_bias, cotangent):
    doms = lax.axis_size("dom")
    plane = lax.axis_size("tile") * lax.axis_size("rep")
    subs, centroids, sub_width = codebook.shape
    slots, side = adj_tiles.shape[1:3]
    width = subs * sub_width
    rows = side // doms
    per = slots * rows
    codes = quantizer_codes.T
    book = codebook.transpose(0, 2, 1)
    adj = adj_tiles[0]
    slot_ids = tile_list[0].T
    swap = [(i, i ^ 1) for i in range(doms)]
    cores = [list(range(c, doms, 2)) for c in range(2)]

    spread = call(spread_kernel, "spread", struct((plane, subs, side), BF16), (), (codes,), pin=False)
    all_codes = exchange(spread, PLANE)
    side_rows, bias = call(
        functools.partial(side_kernel, plane), "side",
        (struct((doms, rows + rows // 2, width), BF16), struct((1, width), F32)),
        (slot_ids, tile_count), (codes, cotangent, out_bias.reshape(1, width)),
    )
    parts = call(
        forward_kernel, "forward", struct((doms, per + rows + rows // 2, width), BF16),
        (slot_ids,), (adj, all_codes, book, side_rows), (VM((width, slots * side), F32),),
    )
    parts = exchange(parts, DOM)
    need, dpre, agg, feats, own_codes = call(
        functools.partial(node_kernel, slots), "node",
        (struct((doms, per + rows, width), BF16), struct((side, width), BF16),
         struct((side, width), BF16), struct((width, side), BF16), struct((subs, side), F32)),
        (), (parts, book, w_self, w_neigh, bias), (VM((width, side), F32),),
    )
    need = exchange(need, DOM)
    half = width // plane
    book_half = subs * sub_width // plane
    keep, give = call(
        weights_kernel, "weights",
        (struct((plane + 1, half, width), F32), struct((plane + 1, half, width), F32)), (), (feats, agg, dpre),
    )
    got = lax.ppermute(give, "dom", swap)
    grads = call(
        pair_kernel, "pair", struct((plane, 2 * half + 8, 128), BF16), (), (keep, got)
    )
    own_book = call(
        own_book_kernel, "own_book", struct((subs, sub_width, centroids), F32), (), (dpre, w_self, own_codes)
    )
    piece = 2 * half + 2 * book_half + 8
    part, node_out = call(
        backward_kernel, "backward",
        (struct((plane, piece, 128), BF16), struct((side, width), BF16)),
        (slot_ids,), (need, adj, all_codes, own_book, grads),
        (VM((width, slots * side), F32),), 1,
    )
    part = exchange(part, PLANE)
    part = call(plane_sum_kernel, "plane_sum", struct((doms // 2, 2 * piece - 16, 128), BF16), (), (part,))
    part = exchange(part, "dom", cores)
    part, grad_bias = call(
        z_sum_kernel, "z_sum", (struct((plane, piece - 8, 128), BF16), struct((8, 128), F32)), (), (part,)
    )
    part = exchange(part, PLANE)
    grad_self, grad_neigh, grad_bias, grad_book = call(
        finish_kernel, "finish",
        (struct((width, width), F32), struct((width, width), F32), struct((1, width), F32),
         struct((subs, sub_width, centroids), F32)),
        (), (part, lax.ppermute(part, "dom", swap), grad_bias), (), 4,
    )
    return (node_out, grad_self, grad_neigh, grad_bias.reshape(width), grad_book.transpose(0, 2, 1))


def solution(mesh):
    every = ("dom", "tile", "rep")
    in_specs = (
        P(every, None), P(), P(every, None, None, None), P(every, None, None), P(every),
        P(), P(), P(), P(every, None),
    )
    out_specs = (P(every, None), P(), P(), P(), P())
    return jax.shard_map(body, mesh=mesh, in_specs=in_specs, out_specs=out_specs, check_vma=False)
```

```python
import functools

import jax
import jax.numpy as jnp
from jax import lax
from jax.experimental import pallas as pl
from jax.experimental.pallas import tpu as pltpu
from jax.sharding import PartitionSpec as P

INTERPRET = False
F32 = jnp.float32
BF16 = jnp.bfloat16
VM = pltpu.VMEM
VMEM_LIMIT = 16 << 20
DOM = ("dom",)
PLANE = ("tile", "rep")


def contract(a, b, da, db):
    return lax.dot_general(a, b, (((da,), (db,)), ((), ())), preferred_element_type=F32)


def call(kernel, name, out_shape, scalars, arrays, scratch=(), final=0, pin=True):
    if not INTERPRET:
        arrays = [pltpu.with_memory_space_constraint(a, VM if pin else pltpu.HBM) for a in arrays]
        shapes = out_shape if isinstance(out_shape, tuple) else (out_shape,)
        kept = len(shapes) - final
        shapes = tuple(VM(o.shape, o.dtype) if i < kept else o for i, o in enumerate(shapes))
        out_shape = shapes if isinstance(out_shape, tuple) else shapes[0]
    return pl.pallas_call(
        kernel,
        name=name,
        out_shape=out_shape,
        in_specs=[pl.BlockSpec(memory_space=pltpu.SMEM)] * len(scalars)
        + [pl.BlockSpec(memory_space=VM)] * len(arrays),
        out_specs=jax.tree.map(lambda _: pl.BlockSpec(memory_space=VM), out_shape),
        scratch_shapes=list(scratch),
        compiler_params=pltpu.CompilerParams(vmem_limit_bytes=VMEM_LIMIT),
        interpret=INTERPRET,
    )(*scalars, *arrays)


def struct(shape, dtype):
    return jax.ShapeDtypeStruct(shape, dtype)


def onehot(row, centroid_ids):
    return jnp.where(centroid_ids.astype(BF16) == row.astype(BF16), jnp.ones((), BF16), jnp.zeros((), BF16))


def centroid_iota(centroids, nodes):
    return lax.broadcasted_iota(jnp.int32, (centroids, nodes), 0).astype(F32)


def decode(codes, book_ref, ids, out_ref):
    sub_count, width, _ = book_ref.shape
    for m in range(sub_count):
        hot = onehot(codes[m : m + 1, :], ids)
        out_ref[m * width : (m + 1) * width, :] = jnp.dot(
            book_ref[m], hot, preferred_element_type=F32
        ).astype(out_ref.dtype)


def shifted_eye(count, shift):
    row = lax.broadcasted_iota(jnp.int32, (count, 128), 0)
    lane = lax.broadcasted_iota(jnp.int32, (count, 128), 1)
    return jnp.where(lane == row + shift, 1.0, 0.0).astype(BF16)


def spread_kernel(codes_ref, out_ref):
    out_ref[...] = jnp.broadcast_to(codes_ref[...].astype(F32).astype(BF16)[None], out_ref.shape)


def side_kernel(plane, tl_ref, tc_ref, codes_ref, cot_ref, bias_ref, side_ref, bias_out):
    doms, all_rows, width = side_ref.shape
    rows = all_rows * 2 // 3
    half = rows // 2
    subs, nodes = codes_ref.shape
    slots = tl_ref.shape[1]
    group = 128 // (slots * rows)
    codes = codes_ref[...].astype(F32).astype(BF16)
    first = contract(codes, shifted_eye(subs, 0), 0, 0)
    second = contract(codes, shifted_eye(subs, subs), 0, 0)
    at = lax.broadcasted_iota(jnp.int32, (half, 128), 1)
    at = at - (lax.axis_index("dom") % group) * (slots * rows)
    meta = jnp.zeros((half, 128), jnp.int32)
    for s in range(slots):
        target = tl_ref[0, s] // plane * rows
        here = (at >= s * rows) & (at < (s + 1) * rows)
        live = s < tc_ref[0]
        meta = jnp.where(here, jnp.where(live, target + at - s * rows, nodes), meta)
    meta = meta.astype(F32).astype(BF16)
    for j in range(doms):
        side_ref[j, 0:rows, :] = cot_ref[j * rows : (j + 1) * rows, :]
        pair = first[j * rows : j * rows + half] + second[j * rows + half : (j + 1) * rows]
        side_ref[j, rows:, 0:128] = pair.astype(BF16)
        side_ref[j, rows:, 128:256] = meta
    bias_out[...] = bias_ref[...]


def forward_kernel(tl_ref, adj_ref, codes_ref, book_ref, side_ref, out_ref, feats_ref):
    plane = codes_ref.shape[0]
    doms = out_ref.shape[0]
    slots, side, _ = adj_ref.shape
    rows = side // doms
    codes = jnp.concatenate([codes_ref[tl_ref[1, s] % plane].astype(F32) for s in range(slots)], axis=1)
    decode(codes, book_ref, centroid_iota(book_ref.shape[2], slots * side), feats_ref)
    for s in range(slots):
        feats = feats_ref[:, s * side : (s + 1) * side].astype(BF16)
        prod = contract(adj_ref[s], feats, 1, 1).astype(BF16)
        for j in range(doms):
            out_ref[j, s * rows : (s + 1) * rows, :] = prod[j * rows : (j + 1) * rows, :]
    out_ref[:, slots * rows :, :] = side_ref[...]


def node_kernel(
    slots, got_ref, book_ref, wself_ref, wneigh_ref, bias_ref,
    send_ref, dpre_ref, agg_ref, feats_out, codes_out, feats_ref,
):
    doms, all_rows, width = got_ref.shape
    rows = 2 * all_rows // (2 * slots + 3)
    half = rows // 2
    per = slots * rows
    group = 128 // per
    nodes = doms * rows
    subs = book_ref.shape[0]
    pairs = got_ref[:, per + rows :, 0:128].reshape(doms * half, 128)
    spot = lax.broadcasted_iota(jnp.int32, (doms * half, nodes), 0)
    spot = spot // half * rows + spot % half
    node = lax.broadcasted_iota(jnp.int32, (doms * half, nodes), 1)
    codes = jnp.zeros((subs, nodes), F32)
    for h in range(2):
        part = contract(shifted_eye(subs, h * subs), pairs, 1, 1).astype(BF16)
        place = jnp.where(node == spot + h * half, 1.0, 0.0).astype(BF16)
        codes = codes + jnp.dot(part, place, preferred_element_type=F32)
    codes_out[...] = codes
    decode(codes, book_ref, centroid_iota(book_ref.shape[2], nodes), feats_ref)
    feats = feats_ref[...].astype(BF16)
    feats_out[...] = feats

    row_ids = lax.broadcasted_iota(jnp.int32, (nodes, 128), 0).astype(F32)
    picks = []
    total = jnp.zeros((nodes, width), F32)
    at = per + rows
    for g in range(doms // group):
        meta = got_ref[g * group, at : at + 1, 128:256].astype(F32)
        for b in range(1, group):
            meta = meta + got_ref[g * group + b, at : at + 1, 128:256].astype(F32)
        pick = jnp.where(row_ids == meta, 1.0, 0.0).astype(BF16)
        picks.append(pick)
        terms = got_ref[g * group : (g + 1) * group, 0:per, :].reshape(128, width)
        total = total + jnp.dot(pick, terms, preferred_element_type=F32)
    agg = total.astype(BF16)
    agg_ref[...] = agg
    pre = (
        contract(feats, wself_ref[...], 0, 0)
        + jnp.dot(agg, wneigh_ref[...], preferred_element_type=F32)
        + bias_ref[...]
    )
    gate = 1.0 / (1.0 + jnp.exp(-pre))
    hidden = pre * gate
    inv = lax.rsqrt(jnp.mean(hidden * hidden, axis=-1, keepdims=True) + 1e-05)
    send_ref[:, per:, :] = (hidden * inv).astype(BF16).reshape(doms, rows, width)
    cot = got_ref[:, per : per + rows, :].reshape(nodes, width).astype(F32)
    lean = jnp.mean(cot * hidden, axis=-1, keepdims=True) * (inv * inv * inv)
    dhidden = cot * inv - hidden * lean
    dpre = (dhidden * gate * (1.0 + pre * (1.0 - gate))).astype(BF16)
    dpre_ref[...] = dpre
    dagg = contract(dpre, wneigh_ref[...], 1, 1).astype(BF16)
    for g in range(doms // group):
        need = contract(picks[g], dagg, 0, 0).astype(BF16)
        send_ref[g * group : (g + 1) * group, 0:per, :] = need.reshape(group, per, width)


def halves(write, keep_ref, give_ref):
    core = lax.axis_index("dom") % 2

    @pl.when(core == 0)
    def _():
        write(keep_ref, give_ref)

    @pl.when(core == 1)
    def _():
        write(give_ref, keep_ref)


def weights_kernel(feats_ref, agg_ref, dpre_ref, keep_ref, give_ref):
    dpre = dpre_ref[...]
    pieces, half, width = keep_ref.shape
    pieces = pieces - 1
    grad_self = jnp.dot(feats_ref[...], dpre, preferred_element_type=F32).reshape(pieces, half, width)
    grad_neigh = contract(agg_ref[...], dpre, 0, 0).reshape(pieces, half, width)
    bias = jnp.sum(dpre.astype(F32), axis=0, keepdims=True)
    keep_ref[pieces] = jnp.broadcast_to(bias, (half, width))
    give_ref[pieces] = jnp.broadcast_to(bias, (half, width))

    def write(first_ref, second_ref):
        first_ref[0:pieces] = grad_self
        second_ref[0:pieces] = grad_neigh

    halves(write, keep_ref, give_ref)


def own_book_kernel(dpre_ref, w_ref, codes_ref, book_ref):
    dx = contract(w_ref[...], dpre_ref[...], 1, 1)
    subs, sub_width, centroids = book_ref.shape
    ids = centroid_iota(centroids, codes_ref.shape[1])
    high = dx.astype(BF16)
    low = (dx - high.astype(F32)).astype(BF16)
    for m in range(subs):
        hot = onehot(codes_ref[m : m + 1, :], ids)
        at = slice(m * sub_width, (m + 1) * sub_width)
        book_ref[m] = contract(high[at], hot, 1, 1) + contract(low[at], hot, 1, 1)


def backward_kernel(
    tl_ref, got_ref, adj_ref, codes_ref, own_ref, grads_ref, out_ref, node_ref, dx_ref
):
    slots, side, _ = adj_ref.shape
    subs, sub_width, centroids = own_ref.shape
    doms, all_rows, width = got_ref.shape
    rows = side // doms
    per = slots * rows
    for s in range(slots):
        dagg = got_ref[:, s * rows : (s + 1) * rows, :].reshape(side, width)
        dx_ref[:, s * side : (s + 1) * side] = contract(dagg, adj_ref[s], 0, 0).astype(BF16).astype(F32)
    pieces, base, _ = grads_ref.shape
    base = base - 8
    each = subs // pieces
    out_ref[:, 0:base, :] = grads_ref[:, 0:base, :]
    out_ref[:, base + 2 * each * sub_width :, :] = grads_ref[:, base:, :]
    plane = codes_ref.shape[0]
    ids = centroid_iota(centroids, slots * side)
    codes = jnp.concatenate([codes_ref[tl_ref[1, s] % plane].astype(F32) for s in range(slots)], axis=1)
    for m in range(subs):
        hot = onehot(codes[m : m + 1, :], ids)
        dx = dx_ref[m * sub_width : (m + 1) * sub_width, :].astype(BF16)
        value = own_ref[m] + contract(dx, hot, 1, 1)
        for h in range(2):
            at = base + (2 * (m % each) + h) * sub_width
            out_ref[m // each, at : at + sub_width, :] = value[:, h * 128 : (h + 1) * 128].astype(out_ref.dtype)
    node_ref[...] = got_ref[:, per:, :].reshape(side, width)


def pair_kernel(keep_ref, got_ref, out_ref):
    pieces = out_ref.shape[0]
    half = keep_ref.shape[1]
    grads = keep_ref[0:pieces] + got_ref[0:pieces]
    for h in range(2):
        lanes = slice(h * 128, (h + 1) * 128)
        out_ref[:, h * half : (h + 1) * half, :] = grads[:, :, lanes].astype(out_ref.dtype)
    low = lax.broadcasted_iota(jnp.int32, (8, 128), 0) < 4
    bias = keep_ref[pieces, 0:8, :] + got_ref[pieces, 0:8, :]
    bias = jnp.where(low, bias[:, 0:128], bias[:, 128:256]).astype(out_ref.dtype)
    out_ref[:, 2 * half :, :] = jnp.broadcast_to(bias[None], (pieces, 8, 128))


def plane_sum_kernel(in_ref, out_ref):
    total = jnp.sum(in_ref[...].astype(F32), axis=0)
    tall = out_ref.shape[1]
    rest = total.shape[0] - tall
    out_ref[:, :, 0:128] = jnp.broadcast_to(total[None, 0:tall], (out_ref.shape[0], tall, 128))
    out_ref[:, 0:rest, 128:256] = jnp.broadcast_to(total[None, tall:], (out_ref.shape[0], rest, 128))
    out_ref[:, rest:, 128:256] = jnp.zeros((out_ref.shape[0], tall - rest, 128), F32)


def z_sum_kernel(in_ref, out_ref, bias_ref):
    total = jnp.sum(in_ref[...], axis=0)
    total = jnp.concatenate([total[:, 0:128], total[:, 128:256]], axis=0)
    rows = out_ref.shape[1]
    out_ref[...] = jnp.broadcast_to(total[None, 0:rows].astype(out_ref.dtype), out_ref.shape)
    bias_ref[...] = total[rows : rows + 8]


def finish_kernel(mine_ref, other_ref, bias_ref, self_ref, neigh_ref, bias_out, book_ref):
    pieces = mine_ref.shape[0]
    half = self_ref.shape[0] // pieces
    subs, sub_width, _ = book_ref.shape
    each = subs // pieces
    first = lax.axis_index("dom") % 2 == 0
    mine, other = mine_ref[...].astype(F32), other_ref[...].astype(F32)
    bias = bias_ref[...]
    for h in range(2):
        lanes = slice(h * 128, (h + 1) * 128)
        at = slice(h * half, (h + 1) * half)
        self_ref[:, lanes] = jnp.where(first, mine[:, at], other[:, at]).reshape(self_ref.shape[0], 128)
        neigh_ref[:, lanes] = jnp.where(first, other[:, at], mine[:, at]).reshape(self_ref.shape[0], 128)
        for e in range(each):
            start = 2 * half + (2 * e + h) * sub_width
            book = mine[:, start : start + sub_width] + other[:, start : start + sub_width]
            for j in range(pieces):
                book_ref[j * each + e, :, lanes] = book[j]
        bias_out[:, lanes] = bias[7 * h : 7 * h + 1]


def exchange(x, axes, groups=None):
    return lax.all_to_all(x, axes, split_axis=0, concat_axis=0, tiled=True, axis_index_groups=groups)


def body(quantizer_codes, codebook, adj_tiles, tile_list, tile_count, w_self, w_neigh, out_bias, cotangent):
    doms = lax.axis_size("dom")
    plane = lax.axis_size("tile") * lax.axis_size("rep")
    subs, centroids, sub_width = codebook.shape
    slots, side = adj_tiles.shape[1:3]
    width = subs * sub_width
    rows = side // doms
    per = slots * rows
    codes = quantizer_codes.T
    book = codebook.transpose(0, 2, 1)
    adj = adj_tiles[0]
    slot_ids = tile_list[0].T
    swap = [(i, i ^ 1) for i in range(doms)]
    cores = [list(range(c, doms, 2)) for c in range(2)]

    spread = call(spread_kernel, "spread", struct((plane, subs, side), BF16), (), (codes,), pin=False)
    all_codes = exchange(spread, PLANE)
    side_rows, bias = call(
        functools.partial(side_kernel, plane), "side",
        (struct((doms, rows + rows // 2, width), BF16), struct((1, width), F32)),
        (slot_ids, tile_count), (codes, cotangent, out_bias.reshape(1, width)),
    )
    parts = call(
        forward_kernel, "forward", struct((doms, per + rows + rows // 2, width), BF16),
        (slot_ids,), (adj, all_codes, book, side_rows), (VM((width, slots * side), F32),),
    )
    parts = exchange(parts, DOM)
    need, dpre, agg, feats, own_codes = call(
        functools.partial(node_kernel, slots), "node",
        (struct((doms, per + rows, width), BF16), struct((side, width), BF16),
         struct((side, width), BF16), struct((width, side), BF16), struct((subs, side), F32)),
        (), (parts, book, w_self, w_neigh, bias), (VM((width, side), F32),),
    )
    need = exchange(need, DOM)
    half = width // plane
    book_half = subs * sub_width // plane
    keep, give = call(
        weights_kernel, "weights",
        (struct((plane + 1, half, width), F32), struct((plane + 1, half, width), F32)), (), (feats, agg, dpre),
    )
    got = lax.ppermute(give, "dom", swap)
    grads = call(
        pair_kernel, "pair", struct((plane, 2 * half + 8, 128), BF16), (), (keep, got)
    )
    own_book = call(
        own_book_kernel, "own_book", struct((subs, sub_width, centroids), F32), (), (dpre, w_self, own_codes)
    )
    piece = 2 * half + 2 * book_half + 8
    part, node_out = call(
        backward_kernel, "backward",
        (struct((plane, piece, 128), BF16), struct((side, width), BF16)),
        (slot_ids,), (need, adj, all_codes, own_book, grads),
        (VM((width, slots * side), F32),), 1,
    )
    part = exchange(part, PLANE)
    part = call(plane_sum_kernel, "plane_sum", struct((doms // 2, (piece + 8) // 2, 256), F32), (), (part,))
    part = exchange(part, "dom", cores)
    part, grad_bias = call(
        z_sum_kernel, "z_sum", (struct((plane, piece - 8, 128), BF16), struct((8, 128), F32)), (), (part,)
    )
    part = exchange(part, PLANE)
    grad_self, grad_neigh, grad_bias, grad_book = call(
        finish_kernel, "finish",
        (struct((width, width), F32), struct((width, width), F32), struct((1, width), F32),
         struct((subs, sub_width, centroids), F32)),
        (), (part, lax.ppermute(part, "dom", swap), grad_bias), (), 4,
    )
    return (node_out, grad_self, grad_neigh, grad_bias.reshape(width), grad_book.transpose(0, 2, 1))


def solution(mesh):
    every = ("dom", "tile", "rep")
    in_specs = (
        P(every, None), P(), P(every, None, None, None), P(every, None, None), P(every),
        P(), P(), P(), P(every, None),
    )
    out_specs = (P(every, None), P(), P(), P(), P())
    return jax.shard_map(body, mesh=mesh, in_specs=in_specs, out_specs=out_specs, check_vma=False)
```
